256 devices in a mesh: dom: 64 (over y, z, core), mp: 4 (over x).
Axes of the slice: x: 4, y: 4, z: 8, core: 2. Of those that a mesh axis runs over, the one named last changes fastest.
Arguments:
- vertex_embedding: bfloat16 [32768, 512], P('dom'), may hold values from -6 to 6
- prenorm_mixer_scale: float32 [512], replicated, may hold values from 0.25 to 1.75
- prenorm_perceptron_scale: float32 [512], replicated, may hold values from 0.25 to 1.75
- triple_projector_stack: bfloat16 [3, 512, 512], P(None, None, 'mp'), may hold values from -0.25 to 0.25
- channel_logit_scaling: float32 [8], P('mp'), may hold values from 0.06 to 8
- mixer_final_projector: bfloat16 [512, 512], P('mp'), may hold values from -0.25 to 0.25
- neighbour_mixer_projector: bfloat16 [512, 512], P('mp'), may hold values from -0.25 to 0.25
- expand_projector: bfloat16 [512, 2048], P(None, 'mp'), may hold values from -0.25 to 0.25
- contract_projector: bfloat16 [2048, 512], P('mp'), may hold values from -0.125 to 0.125
- matched_companion: int32 [2, 64], replicated, may hold values from 0 to 63, as said below
- boundary_sender_vertex: int32 [64, 64, 128], P('dom'), may hold values from 0 to 511
- boundary_slot_tally: int32 [64, 64], P('dom'), may hold values from 0 to 128, as said below
- boundary_landing_vertex: int32 [64, 64, 128], P('dom'), may hold values from 0 to 511
- partition_edge_tail: int32 [64, 16384], P('dom'), may hold values from 0 to 511
- partition_edge_sink: int32 [64, 16384], P('dom'), may hold values from 0 to 511
Outputs:
- updated: bfloat16 [32768, 512], P(('dom', 'mp'))
The draws below stay inside these ranges and needn't reach their ends.
Inputs may be any that keep to these rules, and one draw needn't show every extreme that they name: matched_companion[j, b] equals b XOR c_j for one number c_j of each matching; c_0 and c_1 are at least 1 and differ. Slots at and beyond boundary_slot_tally[s, d] of the 128 slots from s to d are unused; the diagonal is 0; the largest entry is 128.
All inputs are finite; a program needn't handle non-finite values.
Results may differ from the reference program's by a relative error of at most 0.012.
The reference program's roundings to bfloat16 on the way count: a program that leaves them out, or rounds other values in their place, can miss the bound.
Values may be sent and summed in bfloat16 or wider, within the bound.
A program may use at most 64 MiB of HBM per device.

```python
import jax
import jax.numpy as jnp
from jax import lax

D = 512
HEADS = 8
HEAD_SIZE = 64
FF = 2048
BLOCK_NODES = 512
CAP = 128
NBD = 1
E_LOC = 16384
NODES = 32768
N_DOM = 64


def draw_matched_companion(key, part):
    block_total = NBD * N_DOM
    first_key, second_key = jax.random.split(jax.random.fold_in(key, 11))
    first_mask = jax.random.randint(first_key, (), NBD, block_total, dtype=jnp.int32)
    second = jax.random.randint(second_key, (), NBD, block_total - 1, dtype=jnp.int32)
    second = second + (second >= first_mask).astype(jnp.int32)
    blocks = jnp.arange(block_total, dtype=jnp.int32)
    return jnp.stack([jnp.bitwise_xor(blocks, first_mask), jnp.bitwise_xor(blocks, second)])


def draw_boundary_slot_tally(key, part):
    level_key, count_key, pick_key, peer_key = jax.random.split(jax.random.fold_in(key, 23), 4)
    levels = jax.random.randint(level_key, (N_DOM, 1), 3, 5, dtype=jnp.int32)
    counts = jax.random.randint(count_key, (N_DOM, N_DOM), 0, CAP + 1, dtype=jnp.int32) * levels // 4
    sources = jnp.arange(N_DOM, dtype=jnp.int32)
    counts = jnp.where(sources[:, None] == sources[None, :], 0, counts)
    chosen = jax.random.randint(pick_key, (), 0, N_DOM, dtype=jnp.int32)
    peer_index = (chosen + 1 + jax.random.randint(peer_key, (), 0, N_DOM - 1, dtype=jnp.int32)) % N_DOM
    return counts.at[chosen, peer_index].set(CAP)


def draw_channel_logit_scaling(key, part):
    uniform_draw = jax.random.uniform(jax.random.fold_in(key, 37), (HEADS,), jnp.float32)
    fraction = uniform_draw
    lower, upper = (0.06, 0.3)
    return jnp.exp(jnp.log(lower) + fraction * (jnp.log(upper) - jnp.log(lower))).astype(jnp.float32)


def touch_ends(values, key, least, largest):
    extent = values.shape
    index_at = [jax.random.randint(jax.random.fold_in(key, axis), (), 0, extent[axis]) for axis in range(len(extent))]
    values = values.at[tuple(index_at)].set(least)
    longest = extent.index(max(extent))
    index_at[longest] = (index_at[longest] + 1) % extent[longest]
    return values.at[tuple(index_at)].set(largest)


def block_scale(rng, shape, pieces, least, top_value):
    gain = 1.0
    for dim, blocks in pieces:
        steps = jax.random.uniform(jax.random.fold_in(jax.random.fold_in(rng, 6), dim), (blocks,), jnp.float32, least / len(pieces), top_value / len(pieces))
        gain = gain * jnp.repeat(jnp.exp(steps), shape[dim] // blocks).reshape((-1,) + (1,) * (len(shape) - 1 - dim))
    return gain


def noise(stream_key, dims, spread, limit, cuts=(), kind=jnp.bfloat16):
    result = jax.random.normal(stream_key, dims, jnp.float32) * spread
    if len(cuts) > 0:
        result = block_scale(stream_key, dims, cuts, -0.22, 0.18) * result
    return jnp.clip(result, min=-limit, max=limit).astype(kind)


def setup_inputs(seed: int = 0) -> dict:
    keys = jax.random.split(jax.random.key(seed), 16)
    return {
        "vertex_embedding": noise(keys[0], (NODES, D), 1.0, 6.0, ((0, 64),)),
        "prenorm_mixer_scale": jnp.clip(1.0 + 0.15 * jax.random.normal(keys[1], (D,), jnp.float32), 0.25, 1.75),
        "prenorm_perceptron_scale": jnp.clip(1.0 + 0.15 * jax.random.normal(keys[2], (D,), jnp.float32), 0.25, 1.75),
        "triple_projector_stack": noise(keys[3], (3, D, D), D ** -0.5, 0.25, ((2, 4),)),
        "channel_logit_scaling": draw_channel_logit_scaling(jax.random.fold_in(keys[15], 71), 0),
        "mixer_final_projector": noise(keys[5], (D, D), D ** -0.5, 0.25, ((0, 4),)),
        "neighbour_mixer_projector": noise(keys[6], (D, D), D ** -0.5, 0.25, ((0, 4),)),
        "expand_projector": noise(keys[7], (D, FF), D ** -0.5, 0.25, ((1, 4),)),
        "contract_projector": noise(keys[8], (FF, D), FF ** -0.5, 0.125, ((0, 4),)),
        "matched_companion": draw_matched_companion(jax.random.fold_in(keys[15], 71), 0),
        "boundary_sender_vertex": touch_ends(jax.random.randint(keys[10], (N_DOM, N_DOM, CAP), 0, NBD * BLOCK_NODES), jax.random.fold_in(keys[10], 1), 0, (NBD * BLOCK_NODES) - 1).astype(jnp.int32),
        "boundary_slot_tally": draw_boundary_slot_tally(jax.random.fold_in(keys[15], 71), 0),
        "boundary_landing_vertex": touch_ends(jax.random.randint(keys[12], (N_DOM, N_DOM, CAP), 0, NBD * BLOCK_NODES), jax.random.fold_in(keys[12], 1), 0, (NBD * BLOCK_NODES) - 1).astype(jnp.int32),
        "partition_edge_tail": touch_ends(jax.random.randint(keys[13], (N_DOM, E_LOC), 0, NBD * BLOCK_NODES), jax.random.fold_in(keys[13], 1), 0, (NBD * BLOCK_NODES) - 1).astype(jnp.int32),
        "partition_edge_sink": touch_ends(jax.random.randint(keys[14], (N_DOM, E_LOC), 0, NBD * BLOCK_NODES), jax.random.fold_in(keys[14], 1), 0, (NBD * BLOCK_NODES) - 1).astype(jnp.int32),
    }


epsilon = 1e-05

def normalize(matrix, scale_gain):
    matrix = matrix.astype(jnp.float32)
    row_mean = lax.optimization_barrier(jnp.mean(matrix, -1, keepdims=True))
    centred = matrix - row_mean
    variance = lax.optimization_barrier(jnp.mean(centred * centred, -1, keepdims=True))
    return (centred * lax.rsqrt(variance + epsilon) * scale_gain).astype(jnp.bfloat16)

def tile_softmax_mixing(asking_vertices, lookup_tensor, content_tensor, channel_logit_scaling):
    affinity_table = jnp.einsum('rhd,shd->hrs', asking_vertices.astype(jnp.float32), lookup_tensor.astype(jnp.float32))
    affinity_table = affinity_table * channel_logit_scaling[:, None, None]
    weights = jax.nn.softmax(affinity_table, axis=-1).astype(jnp.bfloat16)
    attended = jnp.einsum('hrs,shd->rhd', weights.astype(jnp.float32), content_tensor.astype(jnp.float32))
    return attended.astype(jnp.bfloat16)

def reference(vertex_embedding, prenorm_mixer_scale, prenorm_perceptron_scale, triple_projector_stack, channel_logit_scaling, mixer_final_projector, neighbour_mixer_projector, expand_projector, contract_projector, matched_companion, boundary_sender_vertex, boundary_slot_tally, boundary_landing_vertex, partition_edge_tail, partition_edge_sink):
    node_dev = NBD * BLOCK_NODES
    block_total = NBD * N_DOM
    normed = normalize(vertex_embedding, prenorm_mixer_scale)
    asking_vertices = jnp.dot(normed, triple_projector_stack[0], preferred_element_type=jnp.float32).astype(jnp.bfloat16)
    lookup_tensor = jnp.dot(normed, triple_projector_stack[1], preferred_element_type=jnp.float32).astype(jnp.bfloat16)
    content_tensor = jnp.dot(normed, triple_projector_stack[2], preferred_element_type=jnp.float32).astype(jnp.bfloat16)
    asking_groups = asking_vertices.reshape(block_total, BLOCK_NODES, HEADS, HEAD_SIZE)
    key_blocks = lookup_tensor.reshape(block_total, BLOCK_NODES, HEADS, HEAD_SIZE)
    value_blocks = content_tensor.reshape(block_total, BLOCK_NODES, HEADS, HEAD_SIZE)

    def per_block(tile_offset):
        chosen = jnp.stack([tile_offset, matched_companion[0, tile_offset], matched_companion[1, tile_offset]]).astype(jnp.int32)
        partition_lookups = key_blocks[chosen].reshape(3 * BLOCK_NODES, HEADS, HEAD_SIZE)
        partition_contents = value_blocks[chosen].reshape(3 * BLOCK_NODES, HEADS, HEAD_SIZE)
        return tile_softmax_mixing(asking_groups[tile_offset], partition_lookups, partition_contents, channel_logit_scaling)
    attended = lax.map(per_block, jnp.arange(block_total, dtype=jnp.int32)).reshape(NODES, D)
    attn_term = jnp.dot(attended, mixer_final_projector, preferred_element_type=jnp.float32)

    def per_device(device):
        send_list = boundary_sender_vertex[:, device, :]
        live_slots = jnp.arange(CAP, dtype=jnp.int32)[None, :] < boundary_slot_tally[:, device][:, None]
        global_rows = jnp.arange(N_DOM, dtype=jnp.int32)[:, None] * node_dev + send_list
        sent_values = jnp.where(live_slots[..., None], vertex_embedding[global_rows].astype(jnp.float32), 0.0)
        targets = boundary_landing_vertex[device].reshape(-1)
        boundary = jax.ops.segment_sum(sent_values.reshape(-1, D), targets, num_segments=node_dev)
        degree = jax.ops.segment_sum(live_slots.reshape(-1).astype(jnp.float32), targets, num_segments=node_dev)
        own_block = lax.dynamic_slice_in_dim(vertex_embedding, device * node_dev, node_dev, 0)
        local_sum = jax.ops.segment_sum(own_block[partition_edge_tail[device]].astype(jnp.float32), partition_edge_sink[device], num_segments=node_dev)
        degree = degree + jax.ops.segment_sum(jnp.ones((E_LOC,), jnp.float32), partition_edge_sink[device], num_segments=node_dev)
        message = (own_block.astype(jnp.float32) + local_sum + boundary) / (1.0 + degree)[:, None]
        return message.astype(jnp.bfloat16)
    message = lax.map(per_device, jnp.arange(N_DOM, dtype=jnp.int32)).reshape(NODES, D)
    mixed_rows = vertex_embedding.astype(jnp.float32) + attn_term + jnp.dot(message, neighbour_mixer_projector, preferred_element_type=jnp.float32)
    normed_mlp = normalize(mixed_rows, prenorm_perceptron_scale)
    hidden = jax.nn.gelu(jnp.dot(normed_mlp, expand_projector, preferred_element_type=jnp.float32), approximate=False).astype(jnp.bfloat16)
    return (mixed_rows + jnp.dot(hidden, contract_projector, preferred_element_type=jnp.float32)).astype(jnp.bfloat16)
```

```python
import jax
import jax.numpy as jnp
from jax import lax
from jax.experimental import pallas as pl
from jax.experimental.pallas import tpu as pltpu
from jax.sharding import PartitionSpec as P

MESH = pl.DeviceIdType.MESH
BF16, F32, I32 = jnp.bfloat16, jnp.float32, jnp.int32
NY, NZ, NX = 4, 8, 4
ROWS = 512
LANES = 128
CAP = 128
SPLIT = 320
WROWS = 1280
EPSILON = 1e-05
LOG2E = 1.4426950408889634
MESSAGES = 220


class Net:
    def __init__(self, send_sems, recv_sems):
        self.send_sems, self.recv_sems = send_sems, recv_sems
        self.count = 0
        self.open = []
        dom = lax.axis_index("dom")
        self.m = lax.axis_index("mp")
        y, z = lax.div(dom, 2 * NZ), lax.rem(lax.div(dom, 2), NZ)
        self.c = lax.rem(dom, 2)
        self.me = dom
        self.ys = [lax.rem(y + k, NY) for k in range(NY)]
        self.zs = [lax.rem(z + k, NZ) for k in range(NZ)]
        self.ms = [lax.rem(self.m + k, NX) for k in range(NX)]

    def dom(self, dy, dz, other=0):
        core = 1 - self.c if other else self.c
        return (self.ys[dy % NY] * NZ + self.zs[dz % NZ]) * 2 + core

    def at(self, dy, dz, other=0):
        return {"dom": self.dom(dy, dz, other)}

    def along(self, k):
        return {"mp": self.ms[k % NX]}

    def send(self, src, dst, device, landing):
        i = self.count
        self.count += 1
        copy = pltpu.make_async_remote_copy(
            src_ref=src, dst_ref=dst, send_sem=self.send_sems.at[i], recv_sem=self.recv_sems.at[i],
            device_id=device, device_id_type=MESH)
        copy.start()
        self.open.append(copy)
        arrival = pltpu.make_async_remote_copy(
            src_ref=landing, dst_ref=landing, send_sem=self.send_sems.at[i], recv_sem=self.recv_sems.at[i],
            device_id=device, device_id_type=MESH)
        return arrival.wait_recv

    def finish(self):
        for copy in self.open:
            copy.wait_send()


def half(low, high, sign):
    middle = (low + high) // 2
    return (low, middle) if sign > 0 else (middle, high)


class TorusGather:
    def __init__(self, net, blocks):
        self.net, self.blocks = net, blocks
        self.pending = [[] for _ in range(9)]
        self.twins = [[] for _ in range(9)]
        self.got = {}

    def piece(self, block, low, high):
        return self.blocks.at[block, pl.ds(low, high - low), :]

    def have(self, dy, dz, low, high, level):
        key = (dy % NY, dz % NZ)
        self.got[key] = self.got.get(key, 0) + high - low
        if self.got[key] == ROWS:
            net = self.net
            src = self.blocks.at[net.dom(*key)]
            wait = net.send(src, src, net.at(0, 0, 1), self.blocks.at[net.dom(*key, 1)])
            self.twins[level + 1].append(wait)

    def hop(self, axis, sign, step, dy, dz, low, high, level, then):
        net = self.net
        ring = NY if axis == "y" else NZ
        hy, hz = (sign, 0) if axis == "y" else (0, sign)
        if step == ring // 2:
            low, high = half(low, high, sign)
        oy, oz = dy - hy, dz - hz
        src = self.piece(net.dom(dy, dz), low, high)
        wait = net.send(src, src, net.at(hy, hz), self.piece(net.dom(oy, oz), low, high))

        def arrived(now):
            wait()
            if step < ring // 2:
                self.hop(axis, sign, step + 1, oy, oz, low, high, now, then)
            if then is not None:
                for s in (1, -1):
                    self.hop(then, s, 1, oy, oz, low, high, now, None)
            self.have(oy, oz, low, high, now)

        self.pending[level + 1].append(arrived)

    def start(self):
        for s in (1, -1):
            self.hop("y", s, 1, 0, 0, SPLIT, ROWS, 0, "z")
            self.hop("z", s, 1, 0, 0, 0, SPLIT, 0, "y")
        for s in (1, -1):
            self.hop("z", s, 1, 0, 0, SPLIT, ROWS, 0, None)
            self.hop("y", s, 1, 0, 0, 0, SPLIT, 0, None)
        self.have(0, 0, 0, ROWS, 0)

    def events(self, level):
        return [lambda a=a: a(level) for a in self.pending[level]] + self.twins[level]


def normalize(parts, gains):
    parts = [p.astype(F32) for p in parts]
    width = sum(p.shape[1] for p in parts)
    mean = sum(jnp.sum(p, -1, keepdims=True) for p in parts) / width
    parts = [p - mean for p in parts]
    variance = sum(jnp.sum(p * p, -1, keepdims=True) for p in parts) / width
    scale = lax.rsqrt(variance + EPSILON)
    return [(p * scale * g).astype(BF16) for p, g in zip(parts, gains)]


def dot(a, b):
    return jnp.dot(a, b, preferred_element_type=F32)


def dot_nt(a, b):
    return lax.dot_general(a, b, (((1,), (1,)), ((), ())), preferred_element_type=F32)


def erf(x):
    x = jnp.clip(x, -3.832506856900711, 3.832506856900711)
    s = x * x
    top = jnp.full_like(s, 0.00022905065861350646)
    for k in (0.0034082910107109506, 0.050955695062380861, 0.18520832239976145, 1.128379143519084):
        top = top * s + k
    low = jnp.full_like(s, -1.1791602954361697e-7)
    for k in (0.000023547966471313185, 0.0010179625278914885, 0.014070470171167667, 0.11098505178285362,
              0.49746925110067538, 1.0):
        low = low * s + k
    return x * top / low


def one_hot(match):
    return jnp.where(match, 1.0, 0.0).astype(BF16)


def kernel(x_ref, gain1, gain2, wqkv, logit_scale, wf, wn, we, wc, match_ref, sender_ref, landing_ref,
           tail_ref, sink_ref, out_ref,
           blocks, wall, i1, i2, i3, spread, counts_f, counts, counts_in, q_s, k_s, v_s, m_s, l_s, o_s,
           att_s, att_in, bnd_s, bnd_in, picked, xp, send_sems, recv_sems, local_sems):
    net = Net(send_sems, recv_sems)
    m, c = net.m, net.c

    loads = []
    for k, (ref, low, high) in enumerate(((we, 0, 512), (wc, 512, 1024), (wf, 1024, 1152), (wn, 1152, 1280))):
        loads.append(pltpu.make_async_copy(ref, wall.at[m, pl.ds(low, high - low), :], local_sems.at[k]))
        loads[-1].start()

    blocks[net.me] = x_ref[:, pl.ds(pl.multiple_of(m * LANES, LANES), LANES)]
    barrier = pltpu.get_barrier_semaphore()
    peers = ([net.at(0, k) for k in range(1, NZ)] + [net.at(k, 0) for k in range(1, NY)]
             + [net.at(0, 0, 1)] + [net.along(k) for k in range(1, NX)])
    for peer in peers:
        pl.semaphore_signal(barrier, inc=1, device_id=peer, device_id_type=MESH)
    pl.semaphore_wait(barrier, len(peers))

    waits_z = []
    for k in range(1, NZ):
        waits_z.append(net.send(sender_ref.at[:, net.zs[k]], i1.at[NZ - k], net.at(0, k), i1.at[NZ - k]))
    i1[0] = sender_ref[:, net.zs[0]]

    gather = TorusGather(net, blocks)
    gather.start()

    for load in loads:
        load.wait()

    own_low = pl.multiple_of(c * (WROWS // 2), WROWS // 2)

    def rows(low, high):
        return pl.ds(own_low + low, high - low)

    ring_waits = []
    for s in (1, -1):
        src = wall.at[m, rows(0, 640), :]
        ring_waits.append(net.send(src, src, net.along(s), wall.at[net.ms[-s % NX], rows(0, 640), :]))

    gains = gain1[...]

    @pl.loop(0, 4)
    def _(r):
        sl = pl.ds(pl.multiple_of(r * 128, 128), 128)
        normed = normalize([x_ref[sl, :]], [gains])[0]
        q_s[sl, :] = dot(normed, wqkv[0]).astype(BF16)
        k_s[0, sl, :] = dot(normed, wqkv[1]).astype(BF16)
        v_s[0, sl, :] = dot(normed, wqkv[2]).astype(BF16)

    for wait in waits_z:
        wait()
    waits_y = []
    for k in range(1, NY):
        waits_y.append(net.send(i1.at[:, net.ys[k]], i2.at[NY - k], net.at(k, 0), i2.at[NY - k]))
    i2[0] = i1[:, net.ys[0]]

    def count_step(r):
        base = m * 32 + r * 4
        sub = lax.broadcasted_iota(I32, (ROWS, LANES), 0)
        sinks = jnp.concatenate([one_hot(sub == sink_ref[pl.ds(base + k, 1), :]) for k in range(4)], axis=1)
        tails = jnp.concatenate([one_hot(sub == tail_ref[pl.ds(base + k, 1), :]) for k in range(4)], axis=1)
        return dot_nt(sinks, tails)

    def count_chunk(low, high):
        @pl.loop(low, high)
        def _(r):
            counts_f[...] += count_step(r)

    def attend(j):
        lane = lax.broadcasted_iota(I32, (128, LANES), 1)

        @pl.loop(0, 4)
        def _(r):
            sl = pl.ds(pl.multiple_of(r * 128, 128), 128)
            q = q_s[sl, :]
            for h in range(2):
                mine = (lane >= 64) if h else (lane < 64)
                scores = dot_nt(jnp.where(mine, q, jnp.zeros_like(q)), k_s[j]) * (logit_scale[0, h] * LOG2E)
                top = jnp.max(scores, -1, keepdims=True)
                if j == 0:
                    p = jnp.exp2(scores - top)
                    l_s[h, sl, :] = jnp.broadcast_to(jnp.sum(p, -1, keepdims=True), (128, LANES))
                    o_s[h, sl, :] = dot(p.astype(BF16), v_s[j])
                    m_s[h, sl, :] = jnp.broadcast_to(top, (128, LANES))
                else:
                    old = m_s[h, sl, :]
                    new = jnp.maximum(old, top)
                    shrink = jnp.exp2(old - new)
                    p = jnp.exp2(scores - new[:, :1])
                    l_s[h, sl, :] = l_s[h, sl, :] * shrink + jnp.sum(p, -1, keepdims=True)
                    o_s[h, sl, :] = o_s[h, sl, :] * shrink + dot(p.astype(BF16), v_s[j])
                    m_s[h, sl, :] = new

    def spread_lists():
        for t in range(2):
            table = i3[t].reshape(NY * NZ, LANES).T
            for r in range(NY * NZ):
                spread[t, r // NZ, r % NZ] = jnp.broadcast_to(table[:, r:r + 1], (CAP, LANES))

    def land(dz, t):
        lane = lax.broadcasted_iota(I32, (CAP, ROWS), 1)
        sub = lax.broadcasted_iota(I32, (ROWS, LANES), 0)
        zz = lax.rem(net.zs[0] + dz, NZ)
        core = net.c + t - 2 * net.c * t
        targets = []
        for dy in range(NY):
            block = (net.ys[dy] * NZ + zz) * 2 + core
            index = spread[t, dy, dz]
            pick = one_hot(jnp.concatenate([index] * 4, axis=1) == lane)
            picked[pl.ds(dy * CAP, CAP), pl.ds(0, LANES)] = dot(pick, blocks[block]).astype(BF16)
            target = jnp.where(i3[t, dy, dz] >= 0, landing_ref[block], -1)
            targets.append(one_hot(sub == target))
        bnd_s[...] += dot(jnp.concatenate(targets, axis=1), picked[...])

    def land_level(level):
        if 2 <= level <= 6:
            land_pair(level - 2, 0)
        if 3 <= level <= 7:
            land_pair(level - 3, 1)

    def land_pair(dz, t):
        if dz in (0, 4):
            land(dz, t)
        else:
            @pl.loop(0, 2)
            def _(k):
                land(dz + k * (NZ - 2 * dz), t)

    counts_f[...] = jnp.zeros_like(counts_f)
    bnd_s[...] = jnp.zeros_like(bnd_s)
    picked[:, pl.ds(LANES, LANES)] = jnp.ones((ROWS, LANES), BF16)
    count_chunk(0, 2)
    for event in gather.events(1):
        event()
    for wait in waits_y:
        wait()
    other = pl.multiple_of((1 - c) * LANES, LANES)
    wait_twin = net.send(i2.at[:, :, :, pl.ds(other, LANES)], i3.at[1], net.at(0, 0, 1), i3.at[1])
    i3[0] = i2[:, :, :, pl.ds(pl.multiple_of(c * LANES, LANES), LANES)]
    count_chunk(2, 5)
    wait_twin()
    for event in gather.events(2):
        event()
    count_chunk(5, 8)
    counts[...] = counts_f[...].astype(jnp.int16)
    count_waits = []
    for k in range(1, NX):
        count_waits.append(net.send(
            counts.at[pl.ds(pl.multiple_of(net.ms[k] * 128, 128), 128), :], counts_in.at[NX - k],
            net.along(k), counts_in.at[NX - k]))
    counts_in[0] = counts[pl.ds(pl.multiple_of(m * 128, 128), 128), :]
    spread_lists()
    land_level(2)
    for event in gather.events(3):
        event()
    land_level(3)
    attend(0)
    for wait in ring_waits:
        wait()
    ring_second = []
    for s in (1, -1):
        low, high = half(0, 640, s)
        src = wall.at[net.ms[-s % NX], rows(low, high), :]
        ring_second.append(net.send(src, src, net.along(s), wall.at[net.ms[2], rows(low, high), :]))
    twin_low = pl.multiple_of((1 - c) * (WROWS // 2), WROWS // 2)
    twin_waits = []

    def to_twin(k):
        src = wall.at[net.ms[k], rows(0, 640), :]
        twin_waits.append(net.send(src, src, net.at(0, 0, 1), wall.at[net.ms[k], pl.ds(twin_low, 640), :]))

    to_twin(1)
    to_twin(3)
    for level in (4, 5):
        for event in gather.events(level):
            event()
        land_level(level)
    for level in (6, 7):
        for event in gather.events(level):
            event()

    pair_waits = []
    for j in range(2):
        xp[j, m] = blocks[match_ref[j, net.me]]
        src = xp.at[j, m]
        pair_waits.append([net.send(src, src, net.along(k), xp.at[j, net.ms[NX - k]]) for k in range(1, NX)])
    for wait in ring_second:
        wait()
    to_twin(2)
    land_level(6)
    land_level(7)

    final_waits = []
    for k in range(1, NX):
        final_waits.append(net.send(
            bnd_s.at[pl.ds(pl.multiple_of(net.ms[k] * 128, 128), 128), pl.ds(0, LANES)], bnd_in.at[m],
            net.along(k), bnd_in.at[net.ms[NX - k]]))
    own_rows = pl.ds(pl.multiple_of(m * 128, 128), 128)
    bnd_in[m] = bnd_s[own_rows, pl.ds(0, LANES)]

    for wait in count_waits:
        wait()
    total = (counts_in[0].astype(F32) + counts_in[1].astype(F32)
             + counts_in[2].astype(F32) + counts_in[3].astype(F32))
    coarse = total.astype(BF16)
    fine = (total - coarse.astype(F32)).astype(BF16)
    local_sum = dot(coarse, x_ref[...]) + dot(fine, x_ref[...])
    degree = bnd_s[own_rows, pl.ds(LANES, 1)] + jnp.sum(total, -1, keepdims=True)
    x_own = x_ref[own_rows, :].astype(F32)
    base = x_own + local_sum

    for j in range(2):
        for wait in pair_waits[j]:
            wait()

        @pl.loop(0, 4)
        def _(r):
            sl = pl.ds(pl.multiple_of(r * 128, 128), 128)
            normed = normalize([xp[j, k, sl, :] for k in range(NX)],
                               [gain1[:, pl.ds(k * LANES, LANES)] for k in range(NX)])
            normed = jnp.concatenate(normed, axis=1)
            k_s[j + 1, sl, :] = dot(normed, wqkv[1]).astype(BF16)
            v_s[j + 1, sl, :] = dot(normed, wqkv[2]).astype(BF16)

        attend(j + 1)

    lane = lax.broadcasted_iota(I32, (ROWS, LANES), 1)
    att_s[...] = jnp.where(lane < 64, o_s[0] / l_s[0], o_s[1] / l_s[1]).astype(BF16)
    att_waits = []
    for k in range(1, NX):
        att_waits.append(net.send(
            att_s.at[pl.ds(pl.multiple_of(net.ms[k] * 128, 128), 128), :], att_in.at[m],
            net.along(k), att_in.at[net.ms[NX - k]]))
    att_in[m] = att_s[own_rows, :]

    for wait in twin_waits + final_waits:
        wait()
    message = (base + jnp.concatenate([bnd_in[k] for k in range(NX)], axis=1)) / (1.0 + degree)
    message = message.astype(BF16)
    mixed = x_own
    for k in range(NX):
        mixed += dot(message[:, k * 128:(k + 1) * 128], wall[k, pl.ds(1152, 128), :])
    for wait in att_waits:
        wait()
    for k in range(NX):
        mixed += dot(att_in[k], wall[k, pl.ds(1024, 128), :])
    normed = normalize([mixed], [gain2[...]])[0]
    total_s = counts_f.at[pl.ds(0, 128), :]
    total_s[...] = mixed

    @pl.loop(0, NX)
    def _(k):
        hidden = dot(normed, wall[k, pl.ds(0, 512), :])
        hidden = (hidden * 0.5 * (1.0 + erf(hidden * 0.7071067811865476))).astype(BF16)
        total_s[...] += dot(hidden, wall[k, pl.ds(512, 512), :])

    out_ref[...] = total_s[...].astype(BF16)
    net.finish()


def body(vertex_embedding, prenorm_mixer_scale, prenorm_perceptron_scale, triple_projector_stack,
         channel_logit_scaling, mixer_final_projector, neighbour_mixer_projector, expand_projector,
         contract_projector, matched_companion, boundary_sender_vertex, boundary_slot_tally,
         boundary_landing_vertex, partition_edge_tail, partition_edge_sink):
    slot = jnp.arange(CAP, dtype=I32)
    sender = jnp.where(slot[None, :] < boundary_slot_tally[0][:, None], boundary_sender_vertex[0], -1)
    vmem = pl.BlockSpec(memory_space=pltpu.VMEM)
    smem = pl.BlockSpec(memory_space=pltpu.SMEM)
    anywhere = pl.BlockSpec(memory_space=pl.ANY)
    return pl.pallas_call(
        kernel,
        name="layer",
        out_shape=jax.ShapeDtypeStruct((128, 512), BF16),
        in_specs=[vmem, vmem, vmem, vmem, smem, anywhere, anywhere, anywhere, anywhere, smem, vmem, vmem, vmem, vmem],
        out_specs=vmem,
        scratch_shapes=[
            pltpu.VMEM((64, ROWS, LANES), BF16),
            pltpu.VMEM((NX, WROWS, 512), BF16),
            pltpu.VMEM((NZ, NY, 1, 2 * CAP), I32),
            pltpu.VMEM((NY, NZ, 1, 2 * CAP), I32),
            pltpu.VMEM((2, NY, NZ, 1, CAP), I32),
            pltpu.VMEM((2, NY, NZ, CAP, LANES), I32),
            pltpu.VMEM((ROWS, ROWS), F32),
            pltpu.VMEM((ROWS, ROWS), jnp.int16),
            pltpu.VMEM((NX, 128, ROWS), jnp.int16),
            pltpu.VMEM((ROWS, LANES), BF16),
            pltpu.VMEM((3, ROWS, LANES), BF16),
            pltpu.VMEM((3, ROWS, LANES), BF16),
            pltpu.VMEM((2, ROWS, LANES), F32),
            pltpu.VMEM((2, ROWS, LANES), F32),
            pltpu.VMEM((2, ROWS, LANES), F32),
            pltpu.VMEM((ROWS, LANES), BF16),
            pltpu.VMEM((NX, 128, LANES), BF16),
            pltpu.VMEM((ROWS, 2 * LANES), F32),
            pltpu.VMEM((NX, 128, LANES), F32),
            pltpu.VMEM((ROWS, 2 * LANES), BF16),
            pltpu.VMEM((2, NX, ROWS, LANES), BF16),
            pltpu.SemaphoreType.DMA((MESSAGES,)),
            pltpu.SemaphoreType.DMA((MESSAGES,)),
            pltpu.SemaphoreType.DMA((4,)),
        ],
        compiler_params=pltpu.CompilerParams(
            collective_id=0, has_side_effects=True, vmem_limit_bytes=56 << 20),
    )(
        vertex_embedding,
        prenorm_mixer_scale.reshape(1, 512),
        prenorm_perceptron_scale.reshape(1, 512),
        triple_projector_stack,
        channel_logit_scaling.reshape(1, 2),
        mixer_final_projector,
        neighbour_mixer_projector,
        expand_projector,
        contract_projector,
        matched_companion,
        sender.reshape(NY, NZ, 1, 2 * CAP),
        boundary_landing_vertex.reshape(64, 1, CAP),
        partition_edge_tail.reshape(128, LANES),
        partition_edge_sink.reshape(128, LANES),
    )


def solution(mesh):
    return jax.shard_map(
        body,
        mesh=mesh,
        in_specs=(
            P("dom", None),
            P(),
            P(),
            P(None, None, "mp"),
            P("mp"),
            P("mp", None),
            P("mp", None),
            P(None, "mp"),
            P("mp", None),
            P(),
            P("dom", None, None),
            P("dom", None),
            P("dom", None, None),
            P("dom", None),
            P("dom", None),
        ),
        out_specs=P(("dom", "mp"), None),
        check_vma=False,
    )
```

```python
import jax
import jax.numpy as jnp
from jax import lax
from jax.experimental import pallas as pl
from jax.experimental.pallas import tpu as pltpu
from jax.sharding import PartitionSpec as P

MESH = pl.DeviceIdType.MESH
BF16, F32, I32 = jnp.bfloat16, jnp.float32, jnp.int32
NY, NZ, NX = 4, 8, 4
ROWS = 512
LANES = 128
CAP = 128
SPLIT = 320
WROWS = 1280
EPSILON = 1e-05
LOG2E = 1.4426950408889634
MESSAGES = 220


class Net:
    def __init__(self, send_sems, recv_sems):
        self.send_sems, self.recv_sems = send_sems, recv_sems
        self.count = 0
        self.open = []
        dom = lax.axis_index("dom")
        self.m = lax.axis_index("mp")
        y, z = lax.div(dom, 2 * NZ), lax.rem(lax.div(dom, 2), NZ)
        self.c = lax.rem(dom, 2)
        self.me = dom
        self.ys = [lax.rem(y + k, NY) for k in range(NY)]
        self.zs = [lax.rem(z + k, NZ) for k in range(NZ)]
        self.ms = [lax.rem(self.m + k, NX) for k in range(NX)]

    def dom(self, dy, dz, other=0):
        core = 1 - self.c if other else self.c
        return (self.ys[dy % NY] * NZ + self.zs[dz % NZ]) * 2 + core

    def at(self, dy, dz, other=0):
        return {"dom": self.dom(dy, dz, other)}

    def along(self, k):
        return {"mp": self.ms[k % NX]}

    def send(self, src, dst, device, landing):
        i = self.count
        self.count += 1
        copy = pltpu.make_async_remote_copy(
            src_ref=src, dst_ref=dst, send_sem=self.send_sems.at[i], recv_sem=self.recv_sems.at[i],
            device_id=device, device_id_type=MESH)
        copy.start()
        self.open.append(copy)
        arrival = pltpu.make_async_remote_copy(
            src_ref=landing, dst_ref=landing, send_sem=self.send_sems.at[i], recv_sem=self.recv_sems.at[i],
            device_id=device, device_id_type=MESH)
        return arrival.wait_recv

    def finish(self):
        for copy in self.open:
            copy.wait_send()


def half(low, high, sign):
    middle = (low + high) // 2
    return (low, middle) if sign > 0 else (middle, high)


class TorusGather:
    def __init__(self, net, blocks):
        self.net, self.blocks = net, blocks
        self.pending = [[] for _ in range(9)]
        self.twins = [[] for _ in range(9)]
        self.got = {}

    def piece(self, block, low, high):
        return self.blocks.at[block, pl.ds(low, high - low), :]

    def have(self, dy, dz, low, high, level):
        key = (dy % NY, dz % NZ)
        self.got[key] = self.got.get(key, 0) + high - low
        if self.got[key] == ROWS:
            net = self.net
            src = self.blocks.at[net.dom(*key)]
            wait = net.send(src, src, net.at(0, 0, 1), self.blocks.at[net.dom(*key, 1)])
            self.twins[level + 1].append(wait)

    def hop(self, axis, sign, step, dy, dz, low, high, level, then):
        net = self.net
        ring = NY if axis == "y" else NZ
        hy, hz = (sign, 0) if axis == "y" else (0, sign)
        if step == ring // 2:
            low, high = half(low, high, sign)
        oy, oz = dy - hy, dz - hz
        src = self.piece(net.dom(dy, dz), low, high)
        wait = net.send(src, src, net.at(hy, hz), self.piece(net.dom(oy, oz), low, high))

        def arrived(now):
            wait()
            if step < ring // 2:
                self.hop(axis, sign, step + 1, oy, oz, low, high, now, then)
            if then is not None:
                for s in (1, -1):
                    self.hop(then, s, 1, oy, oz, low, high, now, None)
            self.have(oy, oz, low, high, now)

        self.pending[level + 1].append(arrived)

    def start(self):
        for s in (1, -1):
            self.hop("y", s, 1, 0, 0, SPLIT, ROWS, 0, "z")
            self.hop("z", s, 1, 0, 0, 0, SPLIT, 0, "y")
        for s in (1, -1):
            self.hop("z", s, 1, 0, 0, SPLIT, ROWS, 0, None)
            self.hop("y", s, 1, 0, 0, 0, SPLIT, 0, None)
        self.have(0, 0, 0, ROWS, 0)

    def events(self, level):
        return [lambda a=a: a(level) for a in self.pending[level]] + self.twins[level]


def normalize(parts, gains):
    parts = [p.astype(F32) for p in parts]
    width = sum(p.shape[1] for p in parts)
    mean = sum(jnp.sum(p, -1, keepdims=True) for p in parts) / width
    parts = [p - mean for p in parts]
    variance = sum(jnp.sum(p * p, -1, keepdims=True) for p in parts) / width
    scale = lax.rsqrt(variance + EPSILON)
    return [(p * scale * g).astype(BF16) for p, g in zip(parts, gains)]


def dot(a, b):
    return jnp.dot(a, b, preferred_element_type=F32)


def dot_nt(a, b):
    return lax.dot_general(a, b, (((1,), (1,)), ((), ())), preferred_element_type=F32)


def erf(x):
    x = jnp.clip(x, -3.832506856900711, 3.832506856900711)
    s = x * x
    top = jnp.full_like(s, 0.00022905065861350646)
    for k in (0.0034082910107109506, 0.050955695062380861, 0.18520832239976145, 1.128379143519084):
        top = top * s + k
    low = jnp.full_like(s, -1.1791602954361697e-7)
    for k in (0.000023547966471313185, 0.0010179625278914885, 0.014070470171167667, 0.11098505178285362,
              0.49746925110067538, 1.0):
        low = low * s + k
    return x * top / low


def one_hot(match):
    return jnp.where(match, 1.0, 0.0).astype(BF16)


def kernel(x_ref, gain1, gain2, wqkv, logit_scale, wf, wn, we, wc, match_ref, sender_ref, tally_ref, landing_ref,
           tail_ref, sink_ref, out_ref,
           blocks, wall, i0, i1, i2, i3, spread, counts_f, counts, counts_in, q_s, k_s, v_s, m_s, o_s,
           att_s, att_in, bnd_s, bnd_in, picked, xp, send_sems, recv_sems, local_sems):
    net = Net(send_sems, recv_sems)
    m, c = net.m, net.c

    def rows128(k):
        return pl.ds(pl.multiple_of(k * 128, 128), 128)

    own_rows = rows128(m)

    loads = []
    for k, (ref, low, high) in enumerate(((we, 0, 512), (wc, 512, 1024), (wf, 1024, 1152), (wn, 1152, 1280))):
        loads.append(pltpu.make_async_copy(ref, wall.at[m, pl.ds(low, high - low), :], local_sems.at[k]))
        loads[-1].start()

    blocks[net.me] = x_ref[:, rows128(m)]
    barrier = pltpu.get_barrier_semaphore()
    peers = ([net.at(0, k) for k in range(1, NZ)] + [net.at(k, 0) for k in range(1, NY)]
             + [net.at(0, 0, 1)] + [net.along(k) for k in range(1, NX)])
    for peer in peers:
        pl.semaphore_signal(barrier, inc=1, device_id=peer, device_id_type=MESH)

    lane_row = lax.broadcasted_iota(I32, (1, CAP), 1)
    for d in range(64):
        live = jnp.where(lane_row < tally_ref[0, d], sender_ref[d], -1)
        i0[d // 16, (d // 2) % 8, :, pl.ds((d % 2) * CAP, CAP)] = live
    pl.semaphore_wait(barrier, len(peers))

    waits_z = []
    for k in range(1, NZ):
        waits_z.append(net.send(i0.at[:, net.zs[k]], i1.at[NZ - k], net.at(0, k), i1.at[NZ - k]))
    i1[0] = i0[:, net.zs[0]]

    gather = TorusGather(net, blocks)
    gather.start()

    for load in loads:
        load.wait()

    own_low = pl.multiple_of(c * (WROWS // 2), WROWS // 2)

    def rows(low, high):
        return pl.ds(own_low + low, high - low)

    ring_waits = []
    for s in (1, -1):
        src = wall.at[m, rows(0, 640), :]
        ring_waits.append(net.send(src, src, net.along(s), wall.at[net.ms[-s % NX], rows(0, 640), :]))

    lane128 = lax.broadcasted_iota(I32, (128, LANES), 1)

    def put_values(j, sl, values):
        values = values.astype(BF16)
        ones = jnp.ones_like(values)
        v_s[0, j, sl, :] = jnp.where(lane128 < 64, values, ones)
        v_s[1, j, sl, :] = jnp.where(lane128 < 64, ones, values)

    def project(low, high):
        @pl.loop(low, high)
        def _(r):
            sl = rows128(r)
            normed = normalize([x_ref[sl, :]], [gain1[...]])[0]
            q_s[sl, :] = dot(normed, wqkv[0]).astype(BF16)
            k_s[0, sl, :] = dot(normed, wqkv[1]).astype(BF16)
            put_values(0, sl, dot(normed, wqkv[2]))

    def pair_project(j):
        @pl.loop(0, 4)
        def _(r):
            sl = rows128(r)
            normed = normalize([xp[j, k, sl, :] for k in range(NX)],
                               [gain1[:, pl.ds(k * LANES, LANES)] for k in range(NX)])
            normed = jnp.concatenate(normed, axis=1)
            k_s[j + 1, sl, :] = dot(normed, wqkv[1]).astype(BF16)
            put_values(j + 1, sl, dot(normed, wqkv[2]))

    def count_chunk(low, high):
        @pl.loop(low, high)
        def _(r):
            base = m * 32 + r * 4
            sub = lax.broadcasted_iota(I32, (ROWS, LANES), 0)
            sinks = jnp.concatenate([one_hot(sub == sink_ref[pl.ds(base + k, 1), :]) for k in range(4)], axis=1)
            tails = jnp.concatenate([one_hot(sub == tail_ref[pl.ds(base + k, 1), :]) for k in range(4)], axis=1)
            counts_f[...] += dot_nt(sinks, tails)

    count_waits = []

    def count_send():
        counts[...] = counts_f[...].astype(jnp.int16)
        for k in (2, 1, 3):
            count_waits.append(net.send(
                counts.at[rows128(net.ms[k]), :], counts_in.at[NX - k], net.along(k), counts_in.at[NX - k]))
        counts_in[0] = counts[own_rows, :]

    def attend_rows(j, sl):
        q = q_s[sl, :]
        for h in range(2):
            mine = (lane128 >= 64) if h else (lane128 < 64)
            scores = dot_nt(jnp.where(mine, q, jnp.zeros_like(q)), k_s[j]) * (logit_scale[0, h] * LOG2E)
            top = jnp.max(scores, -1, keepdims=True)
            if j == 0:
                p = jnp.exp2(scores - top)
                o_s[h, sl, :] = dot(p.astype(BF16), v_s[h, j])
                m_s[h, sl, :] = jnp.broadcast_to(top, (128, LANES))
            else:
                old = m_s[h, sl, :]
                new = jnp.maximum(old, top)
                p = jnp.exp2(scores - new[:, :1])
                o_s[h, sl, :] = o_s[h, sl, :] * jnp.exp2(old - new) + dot(p.astype(BF16), v_s[h, j])
                m_s[h, sl, :] = new

    def attend(j):
        @pl.loop(0, 2)
        def _(half):
            for r in range(2):
                attend_rows(j, rows128(half * 2 + r))

    def spread_lists(t):
        table = i3[t].reshape(NY * NZ, LANES).T
        for r in range(NY * NZ):
            spread[t, r // NZ, r % NZ] = jnp.broadcast_to(table[:, r:r + 1], (CAP, LANES))

    def land(dz, t):
        lane = lax.broadcasted_iota(I32, (CAP, ROWS), 1)
        sub = lax.broadcasted_iota(I32, (ROWS, LANES), 0)
        zz = lax.rem(net.zs[0] + dz, NZ)
        core = net.c + t - 2 * net.c * t
        targets = []
        for dy in range(NY):
            block = (net.ys[dy] * NZ + zz) * 2 + core
            index = spread[t, dy, dz]
            pick = one_hot(jnp.concatenate([index] * 4, axis=1) == lane)
            picked[pl.ds(dy * CAP, CAP), pl.ds(0, LANES)] = dot(pick, blocks[block]).astype(BF16)
            target = jnp.where(i3[t, dy, dz] >= 0, landing_ref[block], -1)
            targets.append(one_hot(sub == target))
        bnd_s[...] += dot(jnp.concatenate(targets, axis=1), picked[...])

    def land_pair(dz, t):
        if dz in (0, 4):
            land(dz, t)
        else:
            @pl.loop(0, 2)
            def _(k):
                land(dz + k * (NZ - 2 * dz), t)

    waits_y, wait_c = [], []

    def lists_y():
        for wait in waits_z:
            wait()
        for k in range(1, NY):
            waits_y.append(net.send(i1.at[:, net.ys[k]], i2.at[NY - k], net.at(k, 0), i2.at[NY - k]))
        i2[0] = i1[:, net.ys[0]]

    def lists_c():
        for wait in waits_y:
            wait()
        other = pl.multiple_of((1 - c) * CAP, CAP)
        wait_c.append(net.send(i2.at[:, :, :, pl.ds(other, CAP)], i3.at[1], net.at(0, 0, 1), i3.at[1]))
        i3[0] = i2[:, :, :, pl.ds(pl.multiple_of(c * CAP, CAP), CAP)]

    def lists_end():
        wait_c[0]()

    ring_second, twin_waits = [], []
    twin_low = pl.multiple_of((1 - c) * (WROWS // 2), WROWS // 2)

    def to_twin(k):
        src = wall.at[net.ms[k], rows(0, 640), :]
        twin_waits.append(net.send(src, src, net.at(0, 0, 1), wall.at[net.ms[k], pl.ds(twin_low, 640), :]))

    def weights_second():
        for wait in ring_waits:
            wait()
        for s in (1, -1):
            low, high = half(0, 640, s)
            src = wall.at[net.ms[-s % NX], rows(low, high), :]
            ring_second.append(net.send(src, src, net.along(s), wall.at[net.ms[2], rows(low, high), :]))
        to_twin(1)
        to_twin(3)

    def level(number, tasks=()):
        events = gather.events(number)
        for i, event in enumerate(events):
            event()
            for task in tasks[i * len(tasks) // len(events):(i + 1) * len(tasks) // len(events)]:
                task()

    def run(fn, *args):
        return lambda: fn(*args)

    counts_f[...] = jnp.zeros_like(counts_f)
    bnd_s[...] = jnp.zeros_like(bnd_s)
    picked[:, pl.ds(LANES, LANES)] = jnp.ones((ROWS, LANES), BF16)

    project(0, 2)
    level(1, [run(project, 2, 4)])
    lists_y()
    level(2, [run(count_chunk, k, k + 2) for k in range(0, 8, 2)] + [count_send])
    lists_c()
    level(3, [run(attend, 0), lists_end, run(spread_lists, 0), run(spread_lists, 1),
              run(land_pair, 0, 0)])
    level(4, [run(land_pair, 1, 0), weights_second, run(land_pair, 0, 1)])
    level(5, [run(land_pair, 2, 0), run(land_pair, 1, 1)])
    level(6)
    level(7)

    def exchange(j):
        src = xp.at[j, m]
        return [net.send(src, src, net.along(k), xp.at[j, net.ms[NX - k]]) for k in (2, 1, 3)]

    for j in range(2):
        xp[j, m] = blocks[match_ref[j, net.me]]
    first_pair = exchange(0)
    for dz, t in ((3, 0), (2, 1), (4, 0), (3, 1), (4, 1)):
        land_pair(dz, t)
    for wait in ring_second:
        wait()
    to_twin(2)
    for wait in first_pair:
        wait()
    second_pair = exchange(1)

    final_waits = []
    for k in (2, 1, 3):
        final_waits.append(net.send(bnd_s.at[rows128(net.ms[k]), pl.ds(0, LANES)], bnd_in.at[m],
                                    net.along(k), bnd_in.at[net.ms[NX - k]]))
    bnd_in[m] = bnd_s[own_rows, pl.ds(0, LANES)]

    pair_project(0)
    attend(1)

    for wait in count_waits:
        wait()
    total = (counts_in[0].astype(F32) + counts_in[1].astype(F32)
             + counts_in[2].astype(F32) + counts_in[3].astype(F32))
    coarse = total.astype(BF16)
    fine = (total - coarse.astype(F32)).astype(BF16)
    base_s = counts_f.at[own_rows, :]
    degree = 1.0 + bnd_s[own_rows, pl.ds(LANES, 1)] + jnp.sum(total, -1, keepdims=True)
    base_s[...] = x_ref[own_rows, :].astype(F32) + dot(coarse, x_ref[...]) + dot(fine, x_ref[...])

    for wait in second_pair:
        wait()
    pair_project(1)

    att_waits = []
    for k in (2, 1, 3, 0):
        sl = rows128(net.ms[k])
        attend_rows(2, sl)
        first, second = o_s[0, sl, :], o_s[1, sl, :]
        values = jnp.where(lane128 < 64, first, second)
        sums = jnp.where(lane128 < 64, pltpu.roll(first, 64, 1), pltpu.roll(second, 64, 1))
        attended = (values / sums).astype(BF16)
        if k == 0:
            att_in[m] = attended
        else:
            att_s[sl, :] = attended
            att_waits.append(net.send(att_s.at[sl, :], att_in.at[m], net.along(k), att_in.at[net.ms[NX - k]]))

    for wait in twin_waits + final_waits:
        wait()
    message = (base_s[...] + jnp.concatenate([bnd_in[k] for k in range(NX)], axis=1)) / degree
    message = message.astype(BF16)
    mixed = x_ref[own_rows, :].astype(F32)
    for k in range(NX):
        mixed += dot(message[:, k * 128:(k + 1) * 128], wall[k, pl.ds(1152, 128), :])
    for wait in att_waits:
        wait()
    for k in range(NX):
        mixed += dot(att_in[k], wall[k, pl.ds(1024, 128), :])
    normed = normalize([mixed], [gain2[...]])[0]
    base_s[...] = mixed

    @pl.loop(0, NX)
    def _(k):
        hidden = dot(normed, wall[k, pl.ds(0, 512), :])
        hidden = (hidden * 0.5 * (1.0 + erf(hidden * 0.7071067811865476))).astype(BF16)
        base_s[...] += dot(hidden, wall[k, pl.ds(512, 512), :])

    out_ref[...] = base_s[...].astype(BF16)
    net.finish()


def body(vertex_embedding, prenorm_mixer_scale, prenorm_perceptron_scale, triple_projector_stack,
         channel_logit_scaling, mixer_final_projector, neighbour_mixer_projector, expand_projector,
         contract_projector, matched_companion, boundary_sender_vertex, boundary_slot_tally,
         boundary_landing_vertex, partition_edge_tail, partition_edge_sink):
    vmem = pl.BlockSpec(memory_space=pltpu.VMEM)
    smem = pl.BlockSpec(memory_space=pltpu.SMEM)
    anywhere = pl.BlockSpec(memory_space=pl.ANY)
    return pl.pallas_call(
        kernel,
        name="layer",
        out_shape=jax.ShapeDtypeStruct((128, 512), BF16),
        in_specs=[vmem, vmem, vmem, vmem, smem, anywhere, anywhere, anywhere, anywhere, smem, vmem, smem, vmem, vmem, vmem],
        out_specs=vmem,
        scratch_shapes=[
            pltpu.VMEM((64, ROWS, LANES), BF16),
            pltpu.VMEM((NX, WROWS, 512), BF16),
            pltpu.VMEM((NY, NZ, 1, 2 * CAP), I32),
            pltpu.VMEM((NZ, NY, 1, 2 * CAP), I32),
            pltpu.VMEM((NY, NZ, 1, 2 * CAP), I32),
            pltpu.VMEM((2, NY, NZ, 1, CAP), I32),
            pltpu.VMEM((2, NY, NZ, CAP, LANES), I32),
            pltpu.VMEM((ROWS, ROWS), F32),
            pltpu.VMEM((ROWS, ROWS), jnp.int16),
            pltpu.VMEM((NX, 128, ROWS), jnp.int16),
            pltpu.VMEM((ROWS, LANES), BF16),
            pltpu.VMEM((3, ROWS, LANES), BF16),
            pltpu.VMEM((2, 3, ROWS, LANES), BF16),
            pltpu.VMEM((2, ROWS, LANES), F32),
            pltpu.VMEM((2, ROWS, LANES), F32),
            pltpu.VMEM((ROWS, LANES), BF16),
            pltpu.VMEM((NX, 128, LANES), BF16),
            pltpu.VMEM((ROWS, 2 * LANES), F32),
            pltpu.VMEM((NX, 128, LANES), F32),
            pltpu.VMEM((ROWS, 2 * LANES), BF16),
            pltpu.VMEM((2, NX, ROWS, LANES), BF16),
            pltpu.SemaphoreType.DMA((MESSAGES,)),
            pltpu.SemaphoreType.DMA((MESSAGES,)),
            pltpu.SemaphoreType.DMA((4,)),
        ],
        compiler_params=pltpu.CompilerParams(
            collective_id=0, has_side_effects=True, vmem_limit_bytes=56 << 20),
    )(
        vertex_embedding,
        prenorm_mixer_scale.reshape(1, 512),
        prenorm_perceptron_scale.reshape(1, 512),
        triple_projector_stack,
        channel_logit_scaling.reshape(1, 2),
        mixer_final_projector,
        neighbour_mixer_projector,
        expand_projector,
        contract_projector,
        matched_companion,
        boundary_sender_vertex.reshape(64, 1, CAP),
        boundary_slot_tally,
        boundary_landing_vertex.reshape(64, 1, CAP),
        partition_edge_tail.reshape(128, LANES),
        partition_edge_sink.reshape(128, LANES),
    )


def solution(mesh):
    return jax.shard_map(
        body,
        mesh=mesh,
        in_specs=(
            P("dom", None),
            P(),
            P(),
            P(None, None, "mp"),
            P("mp"),
            P("mp", None),
            P("mp", None),
            P(None, "mp"),
            P("mp", None),
            P(),
            P("dom", None, None),
            P("dom", None),
            P("dom", None, None),
            P("dom", None),
            P("dom", None),
        ),
        out_specs=P(("dom", "mp"), None),
        check_vma=False,
    )
```

```python
import jax
import jax.numpy as jnp
from jax import lax
from jax.experimental import pallas as pl
from jax.experimental.pallas import tpu as pltpu
from jax.sharding import PartitionSpec as P

MESH = pl.DeviceIdType.MESH
BF16, F32, I32 = jnp.bfloat16, jnp.float32, jnp.int32
NY, NZ, NX = 4, 8, 4
ROWS = 512
LANES = 128
CAP = 128
SPLIT = 320
WROWS = 1280
EPSILON = 1e-05
LOG2E = 1.4426950408889634
MESSAGES = 127


class Net:
    def __init__(self, send_sems, recv_sems):
        self.send_sems, self.recv_sems = send_sems, recv_sems
        self.count = 0
        self.open = []
        dom = lax.axis_index("dom")
        self.m = lax.axis_index("mp")
        y, z = lax.div(dom, 2 * NZ), lax.rem(lax.div(dom, 2), NZ)
        self.c = lax.rem(dom, 2)
        self.me = dom
        self.ys = [lax.rem(y + k, NY) for k in range(NY)]
        self.zs = [lax.rem(z + k, NZ) for k in range(NZ)]
        self.ms = [lax.rem(self.m + k, NX) for k in range(NX)]

    def dom(self, dy, dz, other=0):
        core = 1 - self.c if other else self.c
        return (self.ys[dy % NY] * NZ + self.zs[dz % NZ]) * 2 + core

    def at(self, dy, dz, other=0):
        return {"dom": self.dom(dy, dz, other)}

    def along(self, k):
        return {"mp": self.ms[k % NX]}

    def send(self, src, dst, device, landing):
        i = self.count
        self.count += 1
        copy = pltpu.make_async_remote_copy(
            src_ref=src, dst_ref=dst, send_sem=self.send_sems.at[i], recv_sem=self.recv_sems.at[i],
            device_id=device, device_id_type=MESH)
        copy.start()
        self.open.append(copy)
        arrival = pltpu.make_async_remote_copy(
            src_ref=landing, dst_ref=landing, send_sem=self.send_sems.at[i], recv_sem=self.recv_sems.at[i],
            device_id=device, device_id_type=MESH)
        return arrival.wait_recv

    def finish(self):
        for copy in self.open:
            copy.wait_send()


def half(low, high, sign):
    middle = (low + high) // 2
    return (low, middle) if sign > 0 else (middle, high)


class TorusGather:
    def __init__(self, net, blocks):
        self.net, self.blocks = net, blocks
        self.pending = [[] for _ in range(9)]
        self.twins = [[] for _ in range(9)]
        self.got = {}

    def piece(self, block, low, high):
        return self.blocks.at[block, pl.ds(low, high - low), :]

    def have(self, dy, dz, low, high, level):
        key = (dy % NY, dz % NZ)
        self.got[key] = self.got.get(key, 0) + high - low
        if self.got[key] == ROWS:
            net = self.net
            src = self.blocks.at[net.dom(*key)]
            wait = net.send(src, src, net.at(0, 0, 1), self.blocks.at[net.dom(*key, 1)])
            self.twins[level + 1].append(wait)

    def hop(self, axis, sign, step, dy, dz, low, high, level, then):
        net = self.net
        ring = NY if axis == "y" else NZ
        hy, hz = (sign, 0) if axis == "y" else (0, sign)
        if step == ring // 2:
            if ((dz if axis == "y" else dy) + (1 if then == "z" else 0)) % 2 != (0 if sign > 0 else 1):
                return
        oy, oz = dy - hy, dz - hz
        src = self.piece(net.dom(dy, dz), low, high)
        wait = net.send(src, src, net.at(hy, hz), self.piece(net.dom(oy, oz), low, high))

        def arrived(now):
            wait()
            if step < ring // 2:
                self.hop(axis, sign, step + 1, oy, oz, low, high, now, then)
            if then is not None:
                for s in (1, -1):
                    self.hop(then, s, 1, oy, oz, low, high, now, None)
            self.have(oy, oz, low, high, now)

        self.pending[level + 1].append(arrived)

    def start(self):
        for s in (1, -1):
            self.hop("y", s, 1, 0, 0, SPLIT, ROWS, 0, "z")
            self.hop("z", s, 1, 0, 0, 0, SPLIT, 0, "y")
        for s in (1, -1):
            self.hop("z", s, 1, 0, 0, SPLIT, ROWS, 0, None)
            self.hop("y", s, 1, 0, 0, 0, SPLIT, 0, None)
        self.have(0, 0, 0, ROWS, 0)

    def events(self, level):
        return [lambda a=a: a(level) for a in self.pending[level]] + self.twins[level]


def normalize(parts, gains):
    parts = [p.astype(F32) for p in parts]
    width = sum(p.shape[1] for p in parts)
    mean = sum(jnp.sum(p, -1, keepdims=True) for p in parts) / width
    parts = [p - mean for p in parts]
    variance = sum(jnp.sum(p * p, -1, keepdims=True) for p in parts) / width
    scale = lax.rsqrt(variance + EPSILON)
    return [(p * scale * g).astype(BF16) for p, g in zip(parts, gains)]


def dot(a, b):
    return jnp.dot(a, b, preferred_element_type=F32)


def dot_nt(a, b):
    return lax.dot_general(a, b, (((1,), (1,)), ((), ())), preferred_element_type=F32)


def erf(x):
    x = jnp.clip(x, -3.832506856900711, 3.832506856900711)
    s = x * x
    top = jnp.full_like(s, 0.00022905065861350646)
    for k in (0.0034082910107109506, 0.050955695062380861, 0.18520832239976145, 1.128379143519084):
        top = top * s + k
    low = jnp.full_like(s, -1.1791602954361697e-7)
    for k in (0.000023547966471313185, 0.0010179625278914885, 0.014070470171167667, 0.11098505178285362,
              0.49746925110067538, 1.0):
        low = low * s + k
    return x * top / low


def one_hot(match):
    return jnp.where(match, 1.0, 0.0).astype(BF16)


def kernel(x_ref, gain1, gain2, wqkv, logit_scale, wf, wn, we, wc, match_ref, sender_ref, tally_ref, landing_ref,
           tail_ref, sink_ref, out_ref,
           blocks, wall, i0, i1, i2, i3, spread, counts_f, counts, counts_in, q_s, k_s, v_s, m_s, o_s,
           att_s, att_in, bnd_s, bnd_in, picked, xp, send_sems, recv_sems, local_sems):
    net = Net(send_sems, recv_sems)
    m, c = net.m, net.c

    def rows128(k):
        return pl.ds(pl.multiple_of(k * 128, 128), 128)

    own_rows = rows128(m)

    loads = []
    for k, (ref, low, high) in enumerate(((we, 0, 512), (wc, 512, 1024), (wf, 1024, 1152), (wn, 1152, 1280))):
        loads.append(pltpu.make_async_copy(ref, wall.at[m, pl.ds(low, high - low), :], local_sems.at[k]))
        loads[-1].start()

    blocks[net.me] = x_ref[:, rows128(m)]
    barrier = pltpu.get_barrier_semaphore()
    peers = ([net.at(0, k) for k in range(1, NZ)] + [net.at(k, 0) for k in range(1, NY)]
             + [net.at(0, 0, 1)] + [net.along(k) for k in range(1, NX)])
    for peer in peers:
        pl.semaphore_signal(barrier, inc=1, device_id=peer, device_id_type=MESH)

    lane_row = lax.broadcasted_iota(I32, (1, CAP), 1)
    for d in range(64):
        live = jnp.where(lane_row < tally_ref[0, d], sender_ref[d], -1)
        i0[d // 16, (d // 2) % 8, :, pl.ds((d % 2) * CAP, CAP)] = live
    pl.semaphore_wait(barrier, len(peers))

    waits_z = []
    for k in range(1, NZ):
        waits_z.append(net.send(i0.at[:, net.zs[k]], i1.at[NZ - k], net.at(0, k), i1.at[NZ - k]))
    i1[0] = i0[:, net.zs[0]]

    gather = TorusGather(net, blocks)
    gather.start()

    for load in loads:
        load.wait()

    own_low = pl.multiple_of(c * (WROWS // 2), WROWS // 2)

    def rows(low, high):
        return pl.ds(own_low + low, high - low)

    ring_waits = []
    for s in (1, -1):
        src = wall.at[m, rows(0, 640), :]
        ring_waits.append(net.send(src, src, net.along(s), wall.at[net.ms[-s % NX], rows(0, 640), :]))

    lane128 = lax.broadcasted_iota(I32, (128, LANES), 1)

    def put_values(j, sl, values):
        values = values.astype(BF16)
        ones = jnp.ones_like(values)
        v_s[0, j, sl, :] = jnp.where(lane128 < 64, values, ones)
        v_s[1, j, sl, :] = jnp.where(lane128 < 64, ones, values)

    def project(low, high):
        @pl.loop(low, high)
        def _(r):
            sl = rows128(r)
            normed = normalize([x_ref[sl, :]], [gain1[...]])[0]
            q_s[sl, :] = dot(normed, wqkv[0]).astype(BF16)
            k_s[0, sl, :] = dot(normed, wqkv[1]).astype(BF16)
            put_values(0, sl, dot(normed, wqkv[2]))

    def pair_project(j):
        @pl.loop(0, 4)
        def _(r):
            sl = rows128(r)
            normed = normalize([xp[j, k, sl, :] for k in range(NX)],
                               [gain1[:, pl.ds(k * LANES, LANES)] for k in range(NX)])
            normed = jnp.concatenate(normed, axis=1)
            k_s[j + 1, sl, :] = dot(normed, wqkv[1]).astype(BF16)
            put_values(j + 1, sl, dot(normed, wqkv[2]))

    def count_chunk(low, high):
        @pl.loop(low, high)
        def _(r):
            base = m * 32 + r * 4
            sub = lax.broadcasted_iota(I32, (ROWS, LANES), 0)
            sinks = jnp.concatenate([one_hot(sub == sink_ref[pl.ds(base + k, 1), :]) for k in range(4)], axis=1)
            tails = jnp.concatenate([one_hot(sub == tail_ref[pl.ds(base + k, 1), :]) for k in range(4)], axis=1)
            counts_f[...] += dot_nt(sinks, tails)

    count_waits = []

    def count_send():
        counts[...] = counts_f[...].astype(jnp.int16)
        for k in (2, 1, 3):
            count_waits.append(net.send(
                counts.at[rows128(net.ms[k]), :], counts_in.at[NX - k], net.along(k), counts_in.at[NX - k]))
        counts_in[0] = counts[own_rows, :]

    def attend_rows(j, sl):
        q = q_s[sl, :]
        for h in range(2):
            mine = (lane128 >= 64) if h else (lane128 < 64)
            scores = dot_nt(jnp.where(mine, q, jnp.zeros_like(q)), k_s[j]) * (logit_scale[0, h] * LOG2E)
            top = jnp.max(scores, -1, keepdims=True)
            if j == 0:
                p = jnp.exp2(scores - top)
                o_s[h, sl, :] = dot(p.astype(BF16), v_s[h, j])
                m_s[h, sl, :] = jnp.broadcast_to(top, (128, LANES))
            else:
                old = m_s[h, sl, :]
                new = jnp.maximum(old, top)
                p = jnp.exp2(scores - new[:, :1])
                o_s[h, sl, :] = o_s[h, sl, :] * jnp.exp2(old - new) + dot(p.astype(BF16), v_s[h, j])
                m_s[h, sl, :] = new

    def attend(j):
        @pl.loop(0, 2)
        def _(half):
            for r in range(2):
                attend_rows(j, rows128(half * 2 + r))

    def spread_lists(t):
        table = i3[t].reshape(NY * NZ, LANES).T
        for r in range(NY * NZ):
            spread[t, r // NZ, r % NZ] = jnp.broadcast_to(table[:, r:r + 1], (CAP, LANES))

    def land(dz, t):
        lane = lax.broadcasted_iota(I32, (CAP, ROWS), 1)
        sub = lax.broadcasted_iota(I32, (ROWS, LANES), 0)
        zz = lax.rem(net.zs[0] + dz, NZ)
        core = net.c + t - 2 * net.c * t
        targets = []
        for dy in range(NY):
            block = (net.ys[dy] * NZ + zz) * 2 + core
            index = spread[t, dy, dz]
            pick = one_hot(jnp.concatenate([index] * 4, axis=1) == lane)
            picked[pl.ds(dy * CAP, CAP), pl.ds(0, LANES)] = dot(pick, blocks[block]).astype(BF16)
            target = jnp.where(i3[t, dy, dz] >= 0, landing_ref[block], -1)
            targets.append(one_hot(sub == target))
        bnd_s[...] += dot(jnp.concatenate(targets, axis=1), picked[...])

    def land_pair(dz, t):
        if dz in (0, 4):
            land(dz, t)
        else:
            @pl.loop(0, 2)
            def _(k):
                land(dz + k * (NZ - 2 * dz), t)

    waits_y, wait_c = [], []

    def lists_y():
        for wait in waits_z:
            wait()
        for k in range(1, NY):
            waits_y.append(net.send(i1.at[:, net.ys[k]], i2.at[NY - k], net.at(k, 0), i2.at[NY - k]))
        i2[0] = i1[:, net.ys[0]]

    def lists_c():
        for wait in waits_y:
            wait()
        other = pl.multiple_of((1 - c) * CAP, CAP)
        wait_c.append(net.send(i2.at[:, :, :, pl.ds(other, CAP)], i3.at[1], net.at(0, 0, 1), i3.at[1]))
        i3[0] = i2[:, :, :, pl.ds(pl.multiple_of(c * CAP, CAP), CAP)]

    def lists_end():
        wait_c[0]()

    ring_second, twin_waits = [], []
    twin_low = pl.multiple_of((1 - c) * (WROWS // 2), WROWS // 2)

    def to_twin(k):
        src = wall.at[net.ms[k], rows(0, 640), :]
        twin_waits.append(net.send(src, src, net.at(0, 0, 1), wall.at[net.ms[k], pl.ds(twin_low, 640), :]))

    def weights_second():
        for wait in ring_waits:
            wait()
        for s in (1, -1):
            low, high = half(0, 640, s)
            src = wall.at[net.ms[-s % NX], rows(low, high), :]
            ring_second.append(net.send(src, src, net.along(s), wall.at[net.ms[2], rows(low, high), :]))
        to_twin(1)
        to_twin(3)

    def level(number, tasks=()):
        events = gather.events(number)
        for i, event in enumerate(events):
            event()
            for task in tasks[i * len(tasks) // len(events):(i + 1) * len(tasks) // len(events)]:
                task()

    def run(fn, *args):
        return lambda: fn(*args)

    counts_f[...] = jnp.zeros_like(counts_f)
    bnd_s[...] = jnp.zeros_like(bnd_s)
    picked[:, pl.ds(LANES, LANES)] = jnp.ones((ROWS, LANES), BF16)

    project(0, 2)
    level(1, [run(project, 2, 4)])
    lists_y()
    level(2, [run(count_chunk, k, k + 2) for k in range(0, 8, 2)] + [count_send])
    lists_c()
    level(3, [run(attend, 0), lists_end, run(spread_lists, 0), run(spread_lists, 1),
              run(land_pair, 0, 0)])
    level(4, [run(land_pair, 1, 0), weights_second, run(land_pair, 0, 1)])
    level(5, [run(land_pair, 2, 0), run(land_pair, 1, 1)])
    level(6)
    level(7)

    def exchange(j):
        src = xp.at[j, m]
        return [net.send(src, src, net.along(k), xp.at[j, net.ms[NX - k]]) for k in (2, 1, 3)]

    for j in range(2):
        xp[j, m] = blocks[match_ref[j, net.me]]
    first_pair = exchange(0)
    second_pair = exchange(1)
    for dz, t in ((3, 0), (2, 1), (4, 0), (3, 1), (4, 1)):
        land_pair(dz, t)
    for wait in ring_second:
        wait()
    to_twin(2)
    for wait in first_pair:
        wait()

    final_waits = []
    for k in (2, 1, 3):
        final_waits.append(net.send(bnd_s.at[rows128(net.ms[k]), pl.ds(0, LANES)], bnd_in.at[m],
                                    net.along(k), bnd_in.at[net.ms[NX - k]]))
    bnd_in[m] = bnd_s[own_rows, pl.ds(0, LANES)]

    pair_project(0)
    attend(1)

    for wait in count_waits:
        wait()
    total = (counts_in[0].astype(F32) + counts_in[1].astype(F32)
             + counts_in[2].astype(F32) + counts_in[3].astype(F32))
    coarse = total.astype(BF16)
    fine = (total - coarse.astype(F32)).astype(BF16)
    base_s = counts_f.at[own_rows, :]
    degree = 1.0 + bnd_s[own_rows, pl.ds(LANES, 1)] + jnp.sum(total, -1, keepdims=True)
    base_s[...] = x_ref[own_rows, :].astype(F32) + dot(coarse, x_ref[...]) + dot(fine, x_ref[...])

    for wait in second_pair:
        wait()
    pair_project(1)

    att_waits = []
    for k in (2, 1, 3, 0):
        sl = rows128(net.ms[k])
        attend_rows(2, sl)
        first, second = o_s[0, sl, :], o_s[1, sl, :]
        values = jnp.where(lane128 < 64, first, second)
        sums = jnp.where(lane128 < 64, pltpu.roll(first, 64, 1), pltpu.roll(second, 64, 1))
        attended = (values / sums).astype(BF16)
        if k == 0:
            att_in[m] = attended
        else:
            att_s[sl, :] = attended
            att_waits.append(net.send(att_s.at[sl, :], att_in.at[m], net.along(k), att_in.at[net.ms[NX - k]]))

    for wait in twin_waits + final_waits:
        wait()
    message = (base_s[...] + jnp.concatenate([bnd_in[k] for k in range(NX)], axis=1)) / degree
    message = message.astype(BF16)
    mixed = x_ref[own_rows, :].astype(F32)
    for k in range(NX):
        mixed += dot(message[:, k * 128:(k + 1) * 128], wall[k, pl.ds(1152, 128), :])
    for wait in att_waits:
        wait()
    for k in range(NX):
        mixed += dot(att_in[k], wall[k, pl.ds(1024, 128), :])
    normed = normalize([mixed], [gain2[...]])[0]
    base_s[...] = mixed

    @pl.loop(0, NX)
    def _(k):
        hidden = dot(normed, wall[k, pl.ds(0, 512), :])
        hidden = (hidden * 0.5 * (1.0 + erf(hidden * 0.7071067811865476))).astype(BF16)
        base_s[...] += dot(hidden, wall[k, pl.ds(512, 512), :])

    out_ref[...] = base_s[...].astype(BF16)
    net.finish()


def body(vertex_embedding, prenorm_mixer_scale, prenorm_perceptron_scale, triple_projector_stack,
         channel_logit_scaling, mixer_final_projector, neighbour_mixer_projector, expand_projector,
         contract_projector, matched_companion, boundary_sender_vertex, boundary_slot_tally,
         boundary_landing_vertex, partition_edge_tail, partition_edge_sink):
    vmem = pl.BlockSpec(memory_space=pltpu.VMEM)
    smem = pl.BlockSpec(memory_space=pltpu.SMEM)
    anywhere = pl.BlockSpec(memory_space=pl.ANY)
    return pl.pallas_call(
        kernel,
        name="layer",
        out_shape=jax.ShapeDtypeStruct((128, 512), BF16),
        in_specs=[vmem, vmem, vmem, vmem, smem, anywhere, anywhere, anywhere, anywhere, smem, vmem, smem, vmem, vmem, vmem],
        out_specs=vmem,
        scratch_shapes=[
            pltpu.VMEM((64, ROWS, LANES), BF16),
            pltpu.VMEM((NX, WROWS, 512), BF16),
            pltpu.VMEM((NY, NZ, 1, 2 * CAP), I32),
            pltpu.VMEM((NZ, NY, 1, 2 * CAP), I32),
            pltpu.VMEM((NY, NZ, 1, 2 * CAP), I32),
            pltpu.VMEM((2, NY, NZ, 1, CAP), I32),
            pltpu.VMEM((2, NY, NZ, CAP, LANES), I32),
            pltpu.VMEM((ROWS, ROWS), F32),
            pltpu.VMEM((ROWS, ROWS), jnp.int16),
            pltpu.VMEM((NX, 128, ROWS), jnp.int16),
            pltpu.VMEM((ROWS, LANES), BF16),
            pltpu.VMEM((3, ROWS, LANES), BF16),
            pltpu.VMEM((2, 3, ROWS, LANES), BF16),
            pltpu.VMEM((2, ROWS, LANES), F32),
            pltpu.VMEM((2, ROWS, LANES), F32),
            pltpu.VMEM((ROWS, LANES), BF16),
            pltpu.VMEM((NX, 128, LANES), BF16),
            pltpu.VMEM((ROWS, 2 * LANES), F32),
            pltpu.VMEM((NX, 128, LANES), F32),
            pltpu.VMEM((ROWS, 2 * LANES), BF16),
            pltpu.VMEM((2, NX, ROWS, LANES), BF16),
            pltpu.SemaphoreType.DMA((MESSAGES,)),
            pltpu.SemaphoreType.DMA((MESSAGES,)),
            pltpu.SemaphoreType.DMA((4,)),
        ],
        compiler_params=pltpu.CompilerParams(
            collective_id=0, has_side_effects=True, vmem_limit_bytes=56 << 20),
    )(
        vertex_embedding,
        prenorm_mixer_scale.reshape(1, 512),
        prenorm_perceptron_scale.reshape(1, 512),
        triple_projector_stack,
        channel_logit_scaling.reshape(1, 2),
        mixer_final_projector,
        neighbour_mixer_projector,
        expand_projector,
        contract_projector,
        matched_companion,
        boundary_sender_vertex.reshape(64, 1, CAP),
        boundary_slot_tally,
        boundary_landing_vertex.reshape(64, 1, CAP),
        partition_edge_tail.reshape(128, LANES),
        partition_edge_sink.reshape(128, LANES),
    )


def solution(mesh):
    return jax.shard_map(
        body,
        mesh=mesh,
        in_specs=(
            P("dom", None),
            P(),
            P(),
            P(None, None, "mp"),
            P("mp"),
            P("mp", None),
            P("mp", None),
            P(None, "mp"),
            P("mp", None),
            P(),
            P("dom", None, None),
            P("dom", None),
            P("dom", None, None),
            P("dom", None),
            P("dom", None),
        ),
        out_specs=P(("dom", "mp"), None),
        check_vma=False,
    )
```

```python
import jax
import jax.numpy as jnp
from jax import lax
from jax.experimental import pallas as pl
from jax.experimental.pallas import tpu as pltpu
from jax.sharding import PartitionSpec as P

MESH = pl.DeviceIdType.MESH
BF16, F32, I32 = jnp.bfloat16, jnp.float32, jnp.int32
NY, NZ, NX = 4, 8, 4
ROWS = 512
LANES = 128
CAP = 128
SPLIT = 320
WROWS = 1280
EPSILON = 1e-05
LOG2E = 1.4426950408889634
MESSAGES = 127
POOL = 48


class Net:
    def __init__(self, send_sems, recv_sems):
        self.send_sems, self.recv_sems = send_sems, recv_sems
        self.count = 0
        self.open = []
        dom = lax.axis_index("dom")
        self.m = lax.axis_index("mp")
        y, z = lax.div(dom, 2 * NZ), lax.rem(lax.div(dom, 2), NZ)
        self.c = lax.rem(dom, 2)
        self.me = dom
        self.ys = [lax.rem(y + k, NY) for k in range(NY)]
        self.zs = [lax.rem(z + k, NZ) for k in range(NZ)]
        self.ms = [lax.rem(self.m + k, NX) for k in range(NX)]

    def dom(self, dy, dz, other=0):
        core = 1 - self.c if other else self.c
        return (self.ys[dy % NY] * NZ + self.zs[dz % NZ]) * 2 + core

    def at(self, dy, dz, other=0):
        return {"dom": self.dom(dy, dz, other)}

    def along(self, k):
        return {"mp": self.ms[k % NX]}

    def send(self, src, dst, device, landing):
        i = self.count
        self.count += 1
        if i >= POOL:
            self.open[i - POOL].wait_send()
        copy = pltpu.make_async_remote_copy(
            src_ref=src, dst_ref=dst, send_sem=self.send_sems.at[i % POOL], recv_sem=self.recv_sems.at[i],
            device_id=device, device_id_type=MESH)
        copy.start()
        self.open.append(copy)
        arrival = pltpu.make_async_remote_copy(
            src_ref=landing, dst_ref=landing, send_sem=self.send_sems.at[i % POOL], recv_sem=self.recv_sems.at[i],
            device_id=device, device_id_type=MESH)
        return arrival.wait_recv

    def finish(self):
        for copy in self.open[-POOL:]:
            copy.wait_send()


def half(low, high, sign):
    middle = (low + high) // 2
    return (low, middle) if sign > 0 else (middle, high)


class TorusGather:
    def __init__(self, net, blocks):
        self.net, self.blocks = net, blocks
        self.pending = [[] for _ in range(9)]
        self.twins = [[] for _ in range(9)]
        self.got = {}

    def piece(self, block, low, high):
        return self.blocks.at[block, pl.ds(low, high - low), :]

    def have(self, dy, dz, low, high, level):
        key = (dy % NY, dz % NZ)
        self.got[key] = self.got.get(key, 0) + high - low
        if self.got[key] == ROWS:
            net = self.net
            src = self.blocks.at[net.dom(*key)]
            wait = net.send(src, src, net.at(0, 0, 1), self.blocks.at[net.dom(*key, 1)])
            self.twins[level + 1].append(wait)

    def hop(self, axis, sign, step, dy, dz, low, high, level, then):
        net = self.net
        ring = NY if axis == "y" else NZ
        hy, hz = (sign, 0) if axis == "y" else (0, sign)
        if step == ring // 2:
            if ((dz if axis == "y" else dy) + (1 if then == "z" else 0)) % 2 != (0 if sign > 0 else 1):
                return
        oy, oz = dy - hy, dz - hz
        src = self.piece(net.dom(dy, dz), low, high)
        wait = net.send(src, src, net.at(hy, hz), self.piece(net.dom(oy, oz), low, high))

        def arrived(now):
            wait()
            if step < ring // 2:
                self.hop(axis, sign, step + 1, oy, oz, low, high, now, then)
            if then is not None:
                for s in (1, -1):
                    self.hop(then, s, 1, oy, oz, low, high, now, None)
            self.have(oy, oz, low, high, now)

        self.pending[level + 1].append(arrived)

    def start(self):
        for s in (1, -1):
            self.hop("y", s, 1, 0, 0, SPLIT, ROWS, 0, "z")
            self.hop("z", s, 1, 0, 0, 0, SPLIT, 0, "y")
        for s in (1, -1):
            self.hop("z", s, 1, 0, 0, SPLIT, ROWS, 0, None)
            self.hop("y", s, 1, 0, 0, 0, SPLIT, 0, None)
        self.have(0, 0, 0, ROWS, 0)

    def events(self, level):
        return [lambda a=a: a(level) for a in self.pending[level]] + self.twins[level]


def normalize(parts, gains):
    parts = [p.astype(F32) for p in parts]
    width = sum(p.shape[1] for p in parts)
    mean = sum(jnp.sum(p, -1, keepdims=True) for p in parts) / width
    parts = [p - mean for p in parts]
    variance = sum(jnp.sum(p * p, -1, keepdims=True) for p in parts) / width
    scale = lax.rsqrt(variance + EPSILON)
    return [(p * scale * g).astype(BF16) for p, g in zip(parts, gains)]


def dot(a, b):
    return jnp.dot(a, b, preferred_element_type=F32)


def dot_nt(a, b):
    return lax.dot_general(a, b, (((1,), (1,)), ((), ())), preferred_element_type=F32)


def erf(x):
    x = jnp.clip(x, -3.832506856900711, 3.832506856900711)
    s = x * x
    top = jnp.full_like(s, 0.00022905065861350646)
    for k in (0.0034082910107109506, 0.050955695062380861, 0.18520832239976145, 1.128379143519084):
        top = top * s + k
    low = jnp.full_like(s, -1.1791602954361697e-7)
    for k in (0.000023547966471313185, 0.0010179625278914885, 0.014070470171167667, 0.11098505178285362,
              0.49746925110067538, 1.0):
        low = low * s + k
    return x * top / low


def one_hot(match):
    return jnp.where(match, 1.0, 0.0).astype(BF16)


def kernel(x_ref, gain1, gain2, wqkv, logit_scale, wf, wn, we, wc, match_ref, sender_ref, tally_ref, landing_ref,
           tail_ref, sink_ref, out_ref,
           blocks, wall, i0, i1, i2, i3, spread, counts_f, counts, counts_in, q_s, k_s, v_s, m_s, o_s,
           att_s, att_in, bnd_s, bnd_in, picked, xp, send_sems, recv_sems, local_sems):
    net = Net(send_sems, recv_sems)
    m, c = net.m, net.c

    def rows128(k):
        return pl.ds(pl.multiple_of(k * 128, 128), 128)

    own_rows = rows128(m)

    loads = []
    for k, (ref, low, high) in enumerate(((we, 0, 512), (wc, 512, 1024), (wf, 1024, 1152), (wn, 1152, 1280))):
        loads.append(pltpu.make_async_copy(ref, wall.at[m, pl.ds(low, high - low), :], local_sems.at[k]))
        loads[-1].start()

    blocks[net.me] = x_ref[:, rows128(m)]
    barrier = pltpu.get_barrier_semaphore()
    peers = ([net.at(0, k) for k in range(1, NZ)] + [net.at(k, 0) for k in range(1, NY)]
             + [net.at(0, 0, 1)] + [net.along(k) for k in range(1, NX)])
    for peer in peers:
        pl.semaphore_signal(barrier, inc=1, device_id=peer, device_id_type=MESH)

    lane_row = lax.broadcasted_iota(I32, (1, CAP), 1)
    for d in range(64):
        live = jnp.where(lane_row < tally_ref[0, d], sender_ref[d], -1)
        i0[d // 16, (d // 2) % 8, :, pl.ds((d % 2) * CAP, CAP)] = live
    pl.semaphore_wait(barrier, len(peers))

    waits_z = []
    for k in range(1, NZ):
        waits_z.append(net.send(i0.at[:, net.zs[k]], i1.at[NZ - k], net.at(0, k), i1.at[NZ - k]))
    i1[0] = i0[:, net.zs[0]]

    gather = TorusGather(net, blocks)
    gather.start()

    for load in loads:
        load.wait()

    own_low = pl.multiple_of(c * (WROWS // 2), WROWS // 2)

    def rows(low, high):
        return pl.ds(own_low + low, high - low)

    ring_waits = []
    for s in (1, -1):
        src = wall.at[m, rows(0, 640), :]
        ring_waits.append(net.send(src, src, net.along(s), wall.at[net.ms[-s % NX], rows(0, 640), :]))

    lane128 = lax.broadcasted_iota(I32, (128, LANES), 1)

    def put_values(j, sl, values):
        values = values.astype(BF16)
        ones = jnp.ones_like(values)
        v_s[0, j, sl, :] = jnp.where(lane128 < 64, values, ones)
        v_s[1, j, sl, :] = jnp.where(lane128 < 64, ones, values)

    def project(low, high):
        @pl.loop(low, high)
        def _(r):
            sl = rows128(r)
            normed = normalize([x_ref[sl, :]], [gain1[...]])[0]
            q_s[sl, :] = dot(normed, wqkv[0]).astype(BF16)
            k_s[0, sl, :] = dot(normed, wqkv[1]).astype(BF16)
            put_values(0, sl, dot(normed, wqkv[2]))

    def pair_project(j):
        @pl.loop(0, 4)
        def _(r):
            sl = rows128(r)
            normed = normalize([xp[j, k, sl, :] for k in range(NX)],
                               [gain1[:, pl.ds(k * LANES, LANES)] for k in range(NX)])
            normed = jnp.concatenate(normed, axis=1)
            k_s[j + 1, sl, :] = dot(normed, wqkv[1]).astype(BF16)
            put_values(j + 1, sl, dot(normed, wqkv[2]))

    def count_chunk(low, high):
        @pl.loop(low, high)
        def _(r):
            base = m * 32 + r * 4
            sub = lax.broadcasted_iota(I32, (ROWS, LANES), 0)
            sinks = jnp.concatenate([one_hot(sub == sink_ref[pl.ds(base + k, 1), :]) for k in range(4)], axis=1)
            tails = jnp.concatenate([one_hot(sub == tail_ref[pl.ds(base + k, 1), :]) for k in range(4)], axis=1)
            counts_f[...] += dot_nt(sinks, tails)

    count_waits = []

    def count_send():
        counts[...] = counts_f[...].astype(jnp.int16)
        for k in (2, 1, 3):
            count_waits.append(net.send(
                counts.at[rows128(net.ms[k]), :], counts_in.at[NX - k], net.along(k), counts_in.at[NX - k]))
        counts_in[0] = counts[own_rows, :]

    def attend_rows(j, sl):
        q = q_s[sl, :]
        for h in range(2):
            mine = (lane128 >= 64) if h else (lane128 < 64)
            scores = dot_nt(jnp.where(mine, q, jnp.zeros_like(q)), k_s[j]) * (logit_scale[0, h] * LOG2E)
            top = jnp.max(scores, -1, keepdims=True)
            if j == 0:
                p = jnp.exp2(scores - top)
                o_s[h, sl, :] = dot(p.astype(BF16), v_s[h, j])
                m_s[h, sl, :] = jnp.broadcast_to(top, (128, LANES))
            else:
                old = m_s[h, sl, :]
                new = jnp.maximum(old, top)
                p = jnp.exp2(scores - new[:, :1])
                o_s[h, sl, :] = o_s[h, sl, :] * jnp.exp2(old - new) + dot(p.astype(BF16), v_s[h, j])
                m_s[h, sl, :] = new

    def attend(j):
        @pl.loop(0, 2)
        def _(half):
            for r in range(2):
                attend_rows(j, rows128(half * 2 + r))

    def spread_lists(t):
        table = i3[t].reshape(NY * NZ, LANES).T
        for r in range(NY * NZ):
            spread[t, r // NZ, r % NZ] = jnp.broadcast_to(table[:, r:r + 1], (CAP, LANES))

    def land(dz, t):
        lane = lax.broadcasted_iota(I32, (CAP, ROWS), 1)
        sub = lax.broadcasted_iota(I32, (ROWS, LANES), 0)
        zz = lax.rem(net.zs[0] + dz, NZ)
        core = net.c + t - 2 * net.c * t
        targets = []
        for dy in range(NY):
            block = (net.ys[dy] * NZ + zz) * 2 + core
            index = spread[t, dy, dz]
            pick = one_hot(jnp.concatenate([index] * 4, axis=1) == lane)
            picked[pl.ds(dy * CAP, CAP), pl.ds(0, LANES)] = dot(pick, blocks[block]).astype(BF16)
            target = jnp.where(i3[t, dy, dz] >= 0, landing_ref[block], -1)
            targets.append(one_hot(sub == target))
        bnd_s[...] += dot(jnp.concatenate(targets, axis=1), picked[...])

    def land_pair(dz, t):
        if dz in (0, 4):
            land(dz, t)
        else:
            @pl.loop(0, 2)
            def _(k):
                land(dz + k * (NZ - 2 * dz), t)

    waits_y, wait_c = [], []

    def lists_y():
        for wait in waits_z:
            wait()
        for k in range(1, NY):
            waits_y.append(net.send(i1.at[:, net.ys[k]], i2.at[NY - k], net.at(k, 0), i2.at[NY - k]))
        i2[0] = i1[:, net.ys[0]]

    def lists_c():
        for wait in waits_y:
            wait()
        other = pl.multiple_of((1 - c) * CAP, CAP)
        wait_c.append(net.send(i2.at[:, :, :, pl.ds(other, CAP)], i3.at[1], net.at(0, 0, 1), i3.at[1]))
        i3[0] = i2[:, :, :, pl.ds(pl.multiple_of(c * CAP, CAP), CAP)]

    def lists_end():
        wait_c[0]()

    ring_second, twin_waits = [], []
    twin_low = pl.multiple_of((1 - c) * (WROWS // 2), WROWS // 2)

    def to_twin(k):
        src = wall.at[net.ms[k], rows(0, 640), :]
        twin_waits.append(net.send(src, src, net.at(0, 0, 1), wall.at[net.ms[k], pl.ds(twin_low, 640), :]))

    def weights_second():
        for wait in ring_waits:
            wait()
        for s in (1, -1):
            low, high = half(0, 640, s)
            src = wall.at[net.ms[-s % NX], rows(low, high), :]
            ring_second.append(net.send(src, src, net.along(s), wall.at[net.ms[2], rows(low, high), :]))
        to_twin(1)
        to_twin(3)

    def level(number, tasks=()):
        events = gather.events(number)
        for i, event in enumerate(events):
            event()
            for task in tasks[i * len(tasks) // len(events):(i + 1) * len(tasks) // len(events)]:
                task()

    def run(fn, *args):
        return lambda: fn(*args)

    counts_f[...] = jnp.zeros_like(counts_f)
    bnd_s[...] = jnp.zeros_like(bnd_s)
    picked[:, pl.ds(LANES, LANES)] = jnp.ones((ROWS, LANES), BF16)

    project(0, 2)
    level(1, [run(project, 2, 4)])
    lists_y()
    level(2, [run(count_chunk, k, k + 2) for k in range(0, 8, 2)] + [count_send])
    lists_c()
    level(3, [run(attend, 0), lists_end, run(spread_lists, 0), run(spread_lists, 1),
              run(land_pair, 0, 0)])
    level(4, [run(land_pair, 1, 0), weights_second, run(land_pair, 0, 1)])
    level(5, [run(land_pair, 2, 0), run(land_pair, 1, 1)])
    level(6)
    level(7)

    def exchange(j):
        src = xp.at[j, m]
        return [net.send(src, src, net.along(k), xp.at[j, net.ms[NX - k]]) for k in (2, 1, 3)]

    for j in range(2):
        xp[j, m] = blocks[match_ref[j, net.me]]
    first_pair = exchange(0)
    second_pair = exchange(1)
    for dz, t in ((3, 0), (2, 1), (4, 0), (3, 1), (4, 1)):
        land_pair(dz, t)
    for wait in ring_second:
        wait()
    to_twin(2)
    for wait in first_pair:
        wait()

    final_waits = []
    for k in (2, 1, 3):
        final_waits.append(net.send(bnd_s.at[rows128(net.ms[k]), pl.ds(0, LANES)], bnd_in.at[m],
                                    net.along(k), bnd_in.at[net.ms[NX - k]]))
    bnd_in[m] = bnd_s[own_rows, pl.ds(0, LANES)]

    pair_project(0)
    attend(1)

    for wait in count_waits:
        wait()
    total = (counts_in[0].astype(F32) + counts_in[1].astype(F32)
             + counts_in[2].astype(F32) + counts_in[3].astype(F32))
    coarse = total.astype(BF16)
    fine = (total - coarse.astype(F32)).astype(BF16)
    base_s = counts_f.at[own_rows, :]
    degree = 1.0 + bnd_s[own_rows, pl.ds(LANES, 1)] + jnp.sum(total, -1, keepdims=True)
    base_s[...] = x_ref[own_rows, :].astype(F32) + dot(coarse, x_ref[...]) + dot(fine, x_ref[...])

    for wait in second_pair:
        wait()
    pair_project(1)

    att_waits = []
    for k in (2, 1, 3, 0):
        sl = rows128(net.ms[k])
        attend_rows(2, sl)
        first, second = o_s[0, sl, :], o_s[1, sl, :]
        values = jnp.where(lane128 < 64, first, second)
        sums = jnp.where(lane128 < 64, pltpu.roll(first, 64, 1), pltpu.roll(second, 64, 1))
        attended = (values / sums).astype(BF16)
        if k == 0:
            att_in[m] = attended
        else:
            att_s[sl, :] = attended
            att_waits.append(net.send(att_s.at[sl, :], att_in.at[m], net.along(k), att_in.at[net.ms[NX - k]]))

    for wait in twin_waits + final_waits:
        wait()
    message = (base_s[...] + jnp.concatenate([bnd_in[k] for k in range(NX)], axis=1)) / degree
    message = message.astype(BF16)
    mixed = x_ref[own_rows, :].astype(F32)
    for k in range(NX):
        mixed += dot(message[:, k * 128:(k + 1) * 128], wall[k, pl.ds(1152, 128), :])
    for wait in att_waits:
        wait()
    for k in range(NX):
        mixed += dot(att_in[k], wall[k, pl.ds(1024, 128), :])
    normed = normalize([mixed], [gain2[...]])[0]
    base_s[...] = mixed

    @pl.loop(0, NX)
    def _(k):
        hidden = dot(normed, wall[k, pl.ds(0, 512), :])
        hidden = (hidden * 0.5 * (1.0 + erf(hidden * 0.7071067811865476))).astype(BF16)
        base_s[...] += dot(hidden, wall[k, pl.ds(512, 512), :])

    out_ref[...] = base_s[...].astype(BF16)
    net.finish()


def body(vertex_embedding, prenorm_mixer_scale, prenorm_perceptron_scale, triple_projector_stack,
         channel_logit_scaling, mixer_final_projector, neighbour_mixer_projector, expand_projector,
         contract_projector, matched_companion, boundary_sender_vertex, boundary_slot_tally,
         boundary_landing_vertex, partition_edge_tail, partition_edge_sink):
    vmem = pl.BlockSpec(memory_space=pltpu.VMEM)
    smem = pl.BlockSpec(memory_space=pltpu.SMEM)
    anywhere = pl.BlockSpec(memory_space=pl.ANY)
    return pl.pallas_call(
        kernel,
        name="layer",
        out_shape=jax.ShapeDtypeStruct((128, 512), BF16),
        in_specs=[vmem, vmem, vmem, vmem, smem, anywhere, anywhere, anywhere, anywhere, smem, vmem, smem, vmem, vmem, vmem],
        out_specs=vmem,
        scratch_shapes=[
            pltpu.VMEM((64, ROWS, LANES), BF16),
            pltpu.VMEM((NX, WROWS, 512), BF16),
            pltpu.VMEM((NY, NZ, 1, 2 * CAP), I32),
            pltpu.VMEM((NZ, NY, 1, 2 * CAP), I32),
            pltpu.VMEM((NY, NZ, 1, 2 * CAP), I32),
            pltpu.VMEM((2, NY, NZ, 1, CAP), I32),
            pltpu.VMEM((2, NY, NZ, CAP, LANES), I32),
            pltpu.VMEM((ROWS, ROWS), F32),
            pltpu.VMEM((ROWS, ROWS), jnp.int16),
            pltpu.VMEM((NX, 128, ROWS), jnp.int16),
            pltpu.VMEM((ROWS, LANES), BF16),
            pltpu.VMEM((3, ROWS, LANES), BF16),
            pltpu.VMEM((2, 3, ROWS, LANES), BF16),
            pltpu.VMEM((2, ROWS, LANES), F32),
            pltpu.VMEM((2, ROWS, LANES), F32),
            pltpu.VMEM((ROWS, LANES), BF16),
            pltpu.VMEM((NX, 128, LANES), BF16),
            pltpu.VMEM((ROWS, 2 * LANES), F32),
            pltpu.VMEM((NX, 128, LANES), F32),
            pltpu.VMEM((ROWS, 2 * LANES), BF16),
            pltpu.VMEM((2, NX, ROWS, LANES), BF16),
            pltpu.SemaphoreType.DMA((POOL,)),
            pltpu.SemaphoreType.DMA((MESSAGES,)),
            pltpu.SemaphoreType.DMA((4,)),
        ],
        compiler_params=pltpu.CompilerParams(
            collective_id=0, has_side_effects=True, vmem_limit_bytes=56 << 20),
    )(
        vertex_embedding,
        prenorm_mixer_scale.reshape(1, 512),
        prenorm_perceptron_scale.reshape(1, 512),
        triple_projector_stack,
        channel_logit_scaling.reshape(1, 2),
        mixer_final_projector,
        neighbour_mixer_projector,
        expand_projector,
        contract_projector,
        matched_companion,
        boundary_sender_vertex.reshape(64, 1, CAP),
        boundary_slot_tally,
        boundary_landing_vertex.reshape(64, 1, CAP),
        partition_edge_tail.reshape(128, LANES),
        partition_edge_sink.reshape(128, LANES),
    )


def solution(mesh):
    return jax.shard_map(
        body,
        mesh=mesh,
        in_specs=(
            P("dom", None),
            P(),
            P(),
            P(None, None, "mp"),
            P("mp"),
            P("mp", None),
            P("mp", None),
            P(None, "mp"),
            P("mp", None),
            P(),
            P("dom", None, None),
            P("dom", None),
            P("dom", None, None),
            P("dom", None),
            P("dom", None),
        ),
        out_specs=P(("dom", "mp"), None),
        check_vma=False,
    )
```

```python
import jax
import jax.numpy as jnp
from jax import lax
from jax.experimental import pallas as pl
from jax.experimental.pallas import tpu as pltpu
from jax.sharding import PartitionSpec as P

MESH = pl.DeviceIdType.MESH
BF16, F32, I32 = jnp.bfloat16, jnp.float32, jnp.int32
NY, NZ, NX = 4, 8, 4
ROWS = 512
LANES = 128
CAP = 128
SPLIT = 320
WROWS = 1280
EPSILON = 1e-05
LOG2E = 1.4426950408889634
MESSAGES = 127


class Net:
    def __init__(self, send_sems, recv_sems):
        self.send_sems, self.recv_sems = send_sems, recv_sems
        self.count = 0
        self.open = []
        dom = lax.axis_index("dom")
        self.m = lax.axis_index("mp")
        y, z = lax.div(dom, 2 * NZ), lax.rem(lax.div(dom, 2), NZ)
        self.c = lax.rem(dom, 2)
        self.me = dom
        self.ys = [lax.rem(y + k, NY) for k in range(NY)]
        self.zs = [lax.rem(z + k, NZ) for k in range(NZ)]
        self.ms = [lax.rem(self.m + k, NX) for k in range(NX)]

    def dom(self, dy, dz, other=0):
        core = 1 - self.c if other else self.c
        return (self.ys[dy % NY] * NZ + self.zs[dz % NZ]) * 2 + core

    def at(self, dy, dz, other=0):
        return {"dom": self.dom(dy, dz, other)}

    def along(self, k):
        return {"mp": self.ms[k % NX]}

    def send(self, src, dst, device, landing):
        i = self.count
        self.count += 1
        copy = pltpu.make_async_remote_copy(
            src_ref=src, dst_ref=dst, send_sem=self.send_sems.at[i], recv_sem=self.recv_sems.at[i],
            device_id=device, device_id_type=MESH)
        copy.start()
        self.open.append(copy)
        arrival = pltpu.make_async_remote_copy(
            src_ref=landing, dst_ref=landing, send_sem=self.send_sems.at[i], recv_sem=self.recv_sems.at[i],
            device_id=device, device_id_type=MESH)
        return arrival.wait_recv

    def finish(self):
        for copy in self.open:
            copy.wait_send()


def half(low, high, sign):
    middle = (low + high) // 2
    return (low, middle) if sign > 0 else (middle, high)


class TorusGather:
    def __init__(self, net, blocks):
        self.net, self.blocks = net, blocks
        self.pending = [[] for _ in range(9)]
        self.twins = [[] for _ in range(9)]
        self.got = {}

    def piece(self, block, low, high):
        return self.blocks.at[block, pl.ds(low, high - low), :]

    def have(self, dy, dz, low, high, level):
        key = (dy % NY, dz % NZ)
        self.got[key] = self.got.get(key, 0) + high - low
        if self.got[key] == ROWS:
            net = self.net
            src = self.blocks.at[net.dom(*key)]
            wait = net.send(src, src, net.at(0, 0, 1), self.blocks.at[net.dom(*key, 1)])
            self.twins[level + 1].append(wait)

    def hop(self, axis, sign, step, dy, dz, low, high, level, then):
        net = self.net
        ring = NY if axis == "y" else NZ
        hy, hz = (sign, 0) if axis == "y" else (0, sign)
        if step == ring // 2:
            if ((dz if axis == "y" else dy) + (1 if then == "z" else 0)) % 2 != (0 if sign > 0 else 1):
                return
        oy, oz = dy - hy, dz - hz
        src = self.piece(net.dom(dy, dz), low, high)
        wait = net.send(src, src, net.at(hy, hz), self.piece(net.dom(oy, oz), low, high))

        def arrived(now):
            wait()
            if step < ring // 2:
                self.hop(axis, sign, step + 1, oy, oz, low, high, now, then)
            if then is not None:
                for s in (1, -1):
                    self.hop(then, s, 1, oy, oz, low, high, now, None)
            self.have(oy, oz, low, high, now)

        self.pending[level + 1].append(arrived)

    def start(self):
        for s in (1, -1):
            self.hop("y", s, 1, 0, 0, SPLIT, ROWS, 0, "z")
            self.hop("z", s, 1, 0, 0, 0, SPLIT, 0, "y")
        for s in (1, -1):
            self.hop("z", s, 1, 0, 0, SPLIT, ROWS, 0, None)
            self.hop("y", s, 1, 0, 0, 0, SPLIT, 0, None)
        self.have(0, 0, 0, ROWS, 0)

    def events(self, level):
        return [lambda a=a: a(level) for a in self.pending[level]] + self.twins[level]


def normalize(parts, gains):
    parts = [p.astype(F32) for p in parts]
    width = sum(p.shape[1] for p in parts)
    mean = sum(jnp.sum(p, -1, keepdims=True) for p in parts) / width
    parts = [p - mean for p in parts]
    variance = sum(jnp.sum(p * p, -1, keepdims=True) for p in parts) / width
    scale = lax.rsqrt(variance + EPSILON)
    return [(p * scale * g).astype(BF16) for p, g in zip(parts, gains)]


def dot(a, b):
    return jnp.dot(a, b, preferred_element_type=F32)


def dot_nt(a, b):
    return lax.dot_general(a, b, (((1,), (1,)), ((), ())), preferred_element_type=F32)


def erf(x):
    x = jnp.clip(x, -3.832506856900711, 3.832506856900711)
    s = x * x
    top = jnp.full_like(s, 0.00022905065861350646)
    for k in (0.0034082910107109506, 0.050955695062380861, 0.18520832239976145, 1.128379143519084):
        top = top * s + k
    low = jnp.full_like(s, -1.1791602954361697e-7)
    for k in (0.000023547966471313185, 0.0010179625278914885, 0.014070470171167667, 0.11098505178285362,
              0.49746925110067538, 1.0):
        low = low * s + k
    return x * top / low


def one_hot(match):
    return jnp.where(match, 1.0, 0.0).astype(BF16)


def kernel(x_ref, gain1, gain2, wqkv, logit_scale, wf, wn, we, wc, match_ref, sender_ref, tally_ref, landing_ref,
           tail_ref, sink_ref, out_ref,
           blocks, wall, i0, i1, i2, i3, spread, counts_f, counts, counts_in, q_s, k_s, v_s, m_s, o_s,
           att_s, att_in, bnd_s, bnd_in, picked, xp, send_sems, recv_sems, local_sems):
    net = Net(send_sems, recv_sems)
    m, c = net.m, net.c

    def rows128(k):
        return pl.ds(pl.multiple_of(k * 128, 128), 128)

    own_rows = rows128(m)

    loads = []
    for k, (ref, low, high) in enumerate(((we, 0, 512), (wc, 512, 1024), (wf, 1024, 1152), (wn, 1152, 1280))):
        loads.append(pltpu.make_async_copy(ref, wall.at[m, pl.ds(low, high - low), :], local_sems.at[k]))
        loads[-1].start()

    blocks[net.me] = x_ref[:, rows128(m)]
    barrier = pltpu.get_barrier_semaphore()
    peers = ([net.at(0, k) for k in range(1, NZ)] + [net.at(k, 0) for k in range(1, NY)]
             + [net.at(0, 0, 1)] + [net.along(k) for k in range(1, NX)])
    for peer in peers:
        pl.semaphore_signal(barrier, inc=1, device_id=peer, device_id_type=MESH)

    lane_row = lax.broadcasted_iota(I32, (1, CAP), 1)
    for d in range(64):
        live = jnp.where(lane_row < tally_ref[0, d], sender_ref[d], -1)
        i0[d // 16, (d // 2) % 8, :, pl.ds((d % 2) * CAP, CAP)] = live
    pl.semaphore_wait(barrier, len(peers))

    waits_z = []
    for k in range(1, NZ):
        waits_z.append(net.send(i0.at[:, net.zs[k]], i1.at[NZ - k], net.at(0, k), i1.at[NZ - k]))
    i1[0] = i0[:, net.zs[0]]

    gather = TorusGather(net, blocks)
    gather.start()

    for load in loads:
        load.wait()

    own_low = pl.multiple_of(c * (WROWS // 2), WROWS // 2)

    def rows(low, high):
        return pl.ds(own_low + low, high - low)

    ring_waits = []
    for s in (1, -1):
        src = wall.at[m, rows(0, 640), :]
        ring_waits.append(net.send(src, src, net.along(s), wall.at[net.ms[-s % NX], rows(0, 640), :]))

    lane128 = lax.broadcasted_iota(I32, (128, LANES), 1)

    def put_values(j, sl, values):
        values = values.astype(BF16)
        ones = jnp.ones_like(values)
        v_s[0, j, sl, :] = jnp.where(lane128 < 64, values, ones)
        v_s[1, j, sl, :] = jnp.where(lane128 < 64, ones, values)

    def project(low, high):
        @pl.loop(low, high)
        def _(r):
            sl = rows128(r)
            normed = normalize([x_ref[sl, :]], [gain1[...]])[0]
            q_s[sl, :] = dot(normed, wqkv[0]).astype(BF16)
            k_s[0, sl, :] = dot(normed, wqkv[1]).astype(BF16)
            put_values(0, sl, dot(normed, wqkv[2]))

    def pair_project(j):
        @pl.loop(0, 4)
        def _(r):
            sl = rows128(r)
            normed = normalize([xp[j, k, sl, :] for k in range(NX)],
                               [gain1[:, pl.ds(k * LANES, LANES)] for k in range(NX)])
            normed = jnp.concatenate(normed, axis=1)
            k_s[j + 1, sl, :] = dot(normed, wqkv[1]).astype(BF16)
            put_values(j + 1, sl, dot(normed, wqkv[2]))

    def count_chunk(low, high):
        @pl.loop(low, high)
        def _(r):
            base = m * 32 + r * 4
            sub = lax.broadcasted_iota(I32, (ROWS, LANES), 0)
            sinks = jnp.concatenate([one_hot(sub == sink_ref[pl.ds(base + k, 1), :]) for k in range(4)], axis=1)
            tails = jnp.concatenate([one_hot(sub == tail_ref[pl.ds(base + k, 1), :]) for k in range(4)], axis=1)
            counts_f[...] += dot_nt(sinks, tails)

    count_waits = []

    def count_send():
        counts[...] = counts_f[...].astype(jnp.int16)
        for k in (2, 1, 3):
            count_waits.append(net.send(
                counts.at[rows128(net.ms[k]), :], counts_in.at[NX - k], net.along(k), counts_in.at[NX - k]))
        counts_in[0] = counts[own_rows, :]

    def attend_rows(j, sl):
        q = q_s[sl, :]
        for h in range(2):
            mine = (lane128 >= 64) if h else (lane128 < 64)
            scores = dot_nt(jnp.where(mine, q, jnp.zeros_like(q)), k_s[j]) * (logit_scale[0, h] * LOG2E)
            top = jnp.max(scores, -1, keepdims=True)
            if j == 0:
                p = jnp.exp2(scores - top)
                o_s[h, sl, :] = dot(p.astype(BF16), v_s[h, j])
                m_s[h, sl, :] = jnp.broadcast_to(top, (128, LANES))
            else:
                old = m_s[h, sl, :]
                new = jnp.maximum(old, top)
                p = jnp.exp2(scores - new[:, :1])
                o_s[h, sl, :] = o_s[h, sl, :] * jnp.exp2(old - new) + dot(p.astype(BF16), v_s[h, j])
                m_s[h, sl, :] = new

    def attend(j):
        @pl.loop(0, 2)
        def _(half):
            for r in range(2):
                attend_rows(j, rows128(half * 2 + r))

    def spread_lists(t):
        table = i3[t].reshape(NY * NZ, LANES).T
        for r in range(NY * NZ):
            spread[t, r // NZ, r % NZ] = jnp.broadcast_to(table[:, r:r + 1], (CAP, LANES))

    def land(dz, t):
        lane = lax.broadcasted_iota(I32, (CAP, ROWS), 1)
        sub = lax.broadcasted_iota(I32, (ROWS, LANES), 0)
        zz = lax.rem(net.zs[0] + dz, NZ)
        core = net.c + t - 2 * net.c * t
        targets = []
        for dy in range(NY):
            block = (net.ys[dy] * NZ + zz) * 2 + core
            index = spread[t, dy, dz]
            pick = one_hot(jnp.concatenate([index] * 4, axis=1) == lane)
            picked[pl.ds(dy * CAP, CAP), pl.ds(0, LANES)] = dot(pick, blocks[block]).astype(BF16)
            target = jnp.where(i3[t, dy, dz] >= 0, landing_ref[block], -1)
            targets.append(one_hot(sub == target))
        bnd_s[...] += dot(jnp.concatenate(targets, axis=1), picked[...])

    def land_pair(dz, t):
        if dz in (0, 4):
            land(dz, t)
        else:
            @pl.loop(0, 2)
            def _(k):
                land(dz + k * (NZ - 2 * dz), t)

    waits_y, wait_c = [], []

    def lists_y():
        for wait in waits_z:
            wait()
        for k in range(1, NY):
            waits_y.append(net.send(i1.at[:, net.ys[k]], i2.at[NY - k], net.at(k, 0), i2.at[NY - k]))
        i2[0] = i1[:, net.ys[0]]

    def lists_c():
        for wait in waits_y:
            wait()
        other = pl.multiple_of((1 - c) * CAP, CAP)
        wait_c.append(net.send(i2.at[:, :, :, pl.ds(other, CAP)], i3.at[1], net.at(0, 0, 1), i3.at[1]))
        i3[0] = i2[:, :, :, pl.ds(pl.multiple_of(c * CAP, CAP), CAP)]

    def lists_end():
        wait_c[0]()

    ring_second, twin_waits = [], []
    twin_low = pl.multiple_of((1 - c) * (WROWS // 2), WROWS // 2)

    def to_twin(k):
        src = wall.at[net.ms[k], rows(0, 640), :]
        twin_waits.append(net.send(src, src, net.at(0, 0, 1), wall.at[net.ms[k], pl.ds(twin_low, 640), :]))

    def weights_second():
        for wait in ring_waits:
            wait()
        for s in (1, -1):
            low, high = half(0, 640, s)
            src = wall.at[net.ms[-s % NX], rows(low, high), :]
            ring_second.append(net.send(src, src, net.along(s), wall.at[net.ms[2], rows(low, high), :]))
        to_twin(1)
        to_twin(3)

    def level(number, tasks=()):
        events = gather.events(number)
        for i, event in enumerate(events):
            event()
            for task in tasks[i * len(tasks) // len(events):(i + 1) * len(tasks) // len(events)]:
                task()

    def run(fn, *args):
        return lambda: fn(*args)

    counts_f[...] = jnp.zeros_like(counts_f)
    bnd_s[...] = jnp.zeros_like(bnd_s)
    picked[:, pl.ds(LANES, LANES)] = jnp.ones((ROWS, LANES), BF16)

    project(0, 2)
    level(1, [run(project, 2, 4)])
    lists_y()
    level(2, [run(count_chunk, k, k + 2) for k in range(0, 8, 2)] + [count_send])
    lists_c()
    level(3, [run(attend, 0), lists_end, run(spread_lists, 0), run(spread_lists, 1),
              run(land_pair, 0, 0)])
    level(4, [run(land_pair, 1, 0), weights_second, run(land_pair, 0, 1)])
    level(5, [run(land_pair, 2, 0), run(land_pair, 1, 1)])
    level(6)
    level(7)

    def exchange(j):
        src = xp.at[j, m]
        return [net.send(src, src, net.along(k), xp.at[j, net.ms[NX - k]]) for k in (2, 1, 3)]

    for j in range(2):
        xp[j, m] = blocks[match_ref[j, net.me]]
    first_pair = exchange(0)
    second_pair = exchange(1)
    for dz, t in ((3, 0), (2, 1), (4, 0), (3, 1), (4, 1)):
        land_pair(dz, t)
    for wait in count_waits:
        wait()
    total = (counts_in[0].astype(F32) + counts_in[1].astype(F32)
             + counts_in[2].astype(F32) + counts_in[3].astype(F32))
    coarse = total.astype(BF16)
    fine = (total - coarse.astype(F32)).astype(BF16)
    base_s = counts_f.at[own_rows, :]
    degree = 1.0 + bnd_s[own_rows, pl.ds(LANES, 1)] + jnp.sum(total, -1, keepdims=True)
    base_s[...] = x_ref[own_rows, :].astype(F32) + dot(coarse, x_ref[...]) + dot(fine, x_ref[...])

    for wait in ring_second:
        wait()
    to_twin(2)
    for wait in first_pair:
        wait()

    final_waits = []
    for k in (2, 1, 3):
        final_waits.append(net.send(bnd_s.at[rows128(net.ms[k]), pl.ds(0, LANES)], bnd_in.at[m],
                                    net.along(k), bnd_in.at[net.ms[NX - k]]))
    bnd_in[m] = bnd_s[own_rows, pl.ds(0, LANES)]

    pair_project(0)
    attend(1)

    for wait in second_pair:
        wait()
    pair_project(1)

    att_waits = []
    for k in (2, 1, 3, 0):
        sl = rows128(net.ms[k])
        attend_rows(2, sl)
        first, second = o_s[0, sl, :], o_s[1, sl, :]
        values = jnp.where(lane128 < 64, first, second)
        sums = jnp.where(lane128 < 64, pltpu.roll(first, 64, 1), pltpu.roll(second, 64, 1))
        attended = (values / sums).astype(BF16)
        if k == 0:
            att_in[m] = attended
        else:
            att_s[sl, :] = attended
            att_waits.append(net.send(att_s.at[sl, :], att_in.at[m], net.along(k), att_in.at[net.ms[NX - k]]))

    for wait in twin_waits + final_waits:
        wait()
    message = (base_s[...] + jnp.concatenate([bnd_in[k] for k in range(NX)], axis=1)) / degree
    message = message.astype(BF16)
    mixed = x_ref[own_rows, :].astype(F32)
    for k in range(NX):
        mixed += dot(message[:, k * 128:(k + 1) * 128], wall[k, pl.ds(1152, 128), :])
    for wait in att_waits:
        wait()
    for k in range(NX):
        mixed += dot(att_in[k], wall[k, pl.ds(1024, 128), :])
    normed = normalize([mixed], [gain2[...]])[0]
    base_s[...] = mixed

    @pl.loop(0, NX)
    def _(k):
        hidden = dot(normed, wall[k, pl.ds(0, 512), :])
        hidden = (hidden * 0.5 * (1.0 + erf(hidden * 0.7071067811865476))).astype(BF16)
        base_s[...] += dot(hidden, wall[k, pl.ds(512, 512), :])

    out_ref[...] = base_s[...].astype(BF16)
    net.finish()


def body(vertex_embedding, prenorm_mixer_scale, prenorm_perceptron_scale, triple_projector_stack,
         channel_logit_scaling, mixer_final_projector, neighbour_mixer_projector, expand_projector,
         contract_projector, matched_companion, boundary_sender_vertex, boundary_slot_tally,
         boundary_landing_vertex, partition_edge_tail, partition_edge_sink):
    vmem = pl.BlockSpec(memory_space=pltpu.VMEM)
    smem = pl.BlockSpec(memory_space=pltpu.SMEM)
    anywhere = pl.BlockSpec(memory_space=pl.ANY)
    return pl.pallas_call(
        kernel,
        name="layer",
        out_shape=jax.ShapeDtypeStruct((128, 512), BF16),
        in_specs=[vmem, vmem, vmem, vmem, smem, anywhere, anywhere, anywhere, anywhere, smem, vmem, smem, vmem, vmem, vmem],
        out_specs=vmem,
        scratch_shapes=[
            pltpu.VMEM((64, ROWS, LANES), BF16),
            pltpu.VMEM((NX, WROWS, 512), BF16),
            pltpu.VMEM((NY, NZ, 1, 2 * CAP), I32),
            pltpu.VMEM((NZ, NY, 1, 2 * CAP), I32),
            pltpu.VMEM((NY, NZ, 1, 2 * CAP), I32),
            pltpu.VMEM((2, NY, NZ, 1, CAP), I32),
            pltpu.VMEM((2, NY, NZ, CAP, LANES), I32),
            pltpu.VMEM((ROWS, ROWS), F32),
            pltpu.VMEM((ROWS, ROWS), jnp.int16),
            pltpu.VMEM((NX, 128, ROWS), jnp.int16),
            pltpu.VMEM((ROWS, LANES), BF16),
            pltpu.VMEM((3, ROWS, LANES), BF16),
            pltpu.VMEM((2, 3, ROWS, LANES), BF16),
            pltpu.VMEM((2, ROWS, LANES), F32),
            pltpu.VMEM((2, ROWS, LANES), F32),
            pltpu.VMEM((ROWS, LANES), BF16),
            pltpu.VMEM((NX, 128, LANES), BF16),
            pltpu.VMEM((ROWS, 2 * LANES), F32),
            pltpu.VMEM((NX, 128, LANES), F32),
            pltpu.VMEM((ROWS, 2 * LANES), BF16),
            pltpu.VMEM((2, NX, ROWS, LANES), BF16),
            pltpu.SemaphoreType.DMA((MESSAGES,)),
            pltpu.SemaphoreType.DMA((MESSAGES,)),
            pltpu.SemaphoreType.DMA((4,)),
        ],
        compiler_params=pltpu.CompilerParams(
            collective_id=0, has_side_effects=True, vmem_limit_bytes=56 << 20),
    )(
        vertex_embedding,
        prenorm_mixer_scale.reshape(1, 512),
        prenorm_perceptron_scale.reshape(1, 512),
        triple_projector_stack,
        channel_logit_scaling.reshape(1, 2),
        mixer_final_projector,
        neighbour_mixer_projector,
        expand_projector,
        contract_projector,
        matched_companion,
        boundary_sender_vertex.reshape(64, 1, CAP),
        boundary_slot_tally,
        boundary_landing_vertex.reshape(64, 1, CAP),
        partition_edge_tail.reshape(128, LANES),
        partition_edge_sink.reshape(128, LANES),
    )


def solution(mesh):
    return jax.shard_map(
        body,
        mesh=mesh,
        in_specs=(
            P("dom", None),
            P(),
            P(),
            P(None, None, "mp"),
            P("mp"),
            P("mp", None),
            P("mp", None),
            P(None, "mp"),
            P("mp", None),
            P(),
            P("dom", None, None),
            P("dom", None),
            P("dom", None, None),
            P("dom", None),
            P("dom", None),
        ),
        out_specs=P(("dom", "mp"), None),
        check_vma=False,
    )
```
